256 devices in a mesh: box: 64 (over y, z, core), sib: 4 (over x).
Axes of the slice: x: 4, y: 4, z: 8, core: 2. Of those that a mesh axis runs over, the one named last changes fastest.
Arguments:
- self_blocks: float32 [64, 8, 512, 512], P('box', 'sib'), may hold values from -16 to 96, as said below
- orders: int32 [64, 8, 512], P('box', 'sib'), may hold values from 0 to 511, each once within a row
- interpolation: float32 [64, 8, 128, 384], P('box', 'sib'), may hold values from -0.5 to 0.5
- couplings: bfloat16 [64, 8, 512, 16, 128], P('box', 'sib'), may hold values from -0.19921875 to 0.19921875
- neighbours: int32 [64, 8, 16], P('box', 'sib'), may hold values from 0 to 511, as said below
Outputs:
- updated_couplings: bfloat16 [64, 8, 128, 16, 128], P('box', 'sib')
- parent_matrix: float32 [64, 1024, 1024], P('box', 'sib')
The draws below stay inside these ranges and needn't reach their ends.
Inputs may be any that keep to these rules, and one draw needn't show every extreme that they name: `neighbours`: entries 0 to 3 of each list name distinct other children of the same parent. The other entries name children of other parents whose child number c2 has the same c2 // 2 as the box's own, and whose parent number is the box's own plus (j * 32) // 12 or minus (j * 31) // 12, for j from 1 to 12, counted around the end. For each of these 24 differences, exactly 1 far entries of the 2 boxes on one device name it when 2 * 12 is a multiple of 24, else 1 or 0, with 1 reached. Entries of one list may repeat. `self_blocks`: each block is symmetric positive definite.
All inputs are finite; a program needn't handle non-finite values.
Results may differ from the reference program's by a relative error of at most 0.001.
Values sent between devices are 32-bit elements; how exact they have to be, the bound alone decides.
No kernel may reach another device: no remote copies, remote signals or barrier semaphores. Data moves between devices by JAX's collectives and lax.ppermute only.
A program may use at most 128 MiB of HBM per device.

```python
import math
import jax
import jax.numpy as jnp
from jax import lax

BOXDOF = 512
SKEL = 128
NB = 16
NSIB = 4
CPD = 2
PARENTS = 64
RED = 384
NFAR = 12
PDOF = 1024
REACH = 12


def draw_self_blocks(key, part):

    def one_block(sub_key):
        noise = jax.random.normal(sub_key, (BOXDOF, BOXDOF), jnp.float32)
        gram = jnp.dot(noise, noise.T, precision=lax.Precision.HIGHEST) / BOXDOF
        gram = 0.5 * (gram + gram.T)
        diag_log = jax.random.uniform(jax.random.fold_in(sub_key, 5), (BOXDOF,), jnp.float32, math.log(0.5), math.log(3.0))
        matrix = gram + jnp.diag(jnp.exp(diag_log))
        return matrix
    keys = jax.random.split(jax.random.fold_in(key, 3), PARENTS * 8)
    return lax.map(one_block, keys).reshape(PARENTS, 8, BOXDOF, BOXDOF)


def draw_neighbours(key, part):
    sib_groups = 8 // CPD
    parent_ids = jnp.arange(PARENTS, dtype=jnp.int32)
    child_ids = jnp.arange(8, dtype=jnp.int32)
    sib_keys = jax.random.split(jax.random.fold_in(key, 11), PARENTS * 8)
    sib_perm = jax.vmap(lambda sub_key: jax.random.permutation(sub_key, 7))(sib_keys).astype(jnp.int32)
    sib_perm = sib_perm.reshape(PARENTS, 8, 7)[:, :, :NSIB]
    sib_child = (child_ids[None, :, None] + 1 + sib_perm) % 8
    sib_entries = parent_ids[:, None, None] * 8 + sib_child
    span = 2 * REACH
    steps_up = jnp.arange(1, REACH + 1, dtype=jnp.int32) * (PARENTS // 2) // REACH
    steps_down = jnp.arange(1, REACH + 1, dtype=jnp.int32) * ((PARENTS - 1) // 2) // REACH
    far_keys = jax.random.split(jax.random.fold_in(key, 23), PARENTS * sib_groups)
    far_perm = jax.vmap(lambda sub_key: jax.random.permutation(sub_key, span))(far_keys).astype(jnp.int32)
    far_perm = far_perm.reshape(PARENTS, sib_groups, span)
    slot_index = jnp.arange(CPD * NFAR, dtype=jnp.int32) % span
    picks = jnp.take(far_perm, slot_index, axis=2)
    level = picks // 2
    offsets = jnp.where(picks % 2 == 0, jnp.take(steps_up, level), PARENTS - jnp.take(steps_down, level))
    far_parent = (parent_ids[:, None, None] + offsets) % PARENTS
    local_child = jax.random.randint(jax.random.fold_in(key, 37), (PARENTS, sib_groups, CPD * NFAR), 0, CPD).astype(jnp.int32)
    far_child = jnp.arange(sib_groups, dtype=jnp.int32)[None, :, None] * CPD + local_child
    far_entries = (far_parent * 8 + far_child).reshape(PARENTS, 8, NFAR)
    return jnp.concatenate([sib_entries, far_entries], axis=2).astype(jnp.int32)


def steps_of(key, extent, pieces, smallest, high):
    loudness = 1.0
    for position, parts in pieces:
        draws = jax.random.uniform(jax.random.fold_in(jax.random.fold_in(key, 6), position), (parts,), jnp.float32, smallest / len(pieces), high / len(pieces))
        loudness = loudness * jnp.repeat(jnp.exp(draws), extent[position] // parts).reshape((-1,) + (1,) * (len(extent) - 1 - position))
    return loudness


def normal_values(rng, dims, width, limit, pieces=(), held_as=jnp.bfloat16):
    loudness = steps_of(rng, dims, pieces, -0.22, 0.18) if pieces else 1.0
    entries = jax.random.normal(rng, dims, jnp.float32) * width * loudness
    return jnp.minimum(jnp.maximum(entries, -limit), limit).astype(held_as)


def setup_inputs(seed: int = 0) -> dict:
    splits = jax.random.split(jax.random.key(seed), 6)
    return {
        "self_blocks": draw_self_blocks(jax.random.fold_in(splits[5], 71), 0),
        "orders": jax.vmap(lambda own: jax.random.permutation(own, BOXDOF))(jax.random.split(splits[1], PARENTS * 8)).reshape((PARENTS, 8, BOXDOF)).astype(jnp.int32),
        "interpolation": normal_values(splits[2], (PARENTS, 8, SKEL, RED), SKEL ** -0.5, 0.5, ((0, 64), (1, 4)), jnp.float32),
        "couplings": normal_values(splits[3], (PARENTS, 8, BOXDOF, NB, SKEL), 0.03, 0.19921875, ((0, 64), (1, 4))),
        "neighbours": draw_neighbours(jax.random.fold_in(splits[5], 71), 0),
    }


HIGH = lax.Precision.HIGHEST

def eliminate(operands):
    self_block, ordering, interpolation, coupling = operands
    skeleton = interpolation.shape[0]
    permuted = jnp.take(jnp.take(self_block, ordering, axis=0), ordering, axis=1)
    skel_skel = permuted[:skeleton, :skeleton]
    skel_red = permuted[:skeleton, skeleton:]
    red_red = permuted[skeleton:, skeleton:]
    mixed_term = jnp.dot(interpolation.T, skel_skel, precision=HIGH)
    cross_term = jnp.dot(interpolation.T, skel_red, precision=HIGH)
    bar_skel_red = skel_red - jnp.dot(skel_skel, interpolation, precision=HIGH)
    bar_red_red = red_red - cross_term - cross_term.T + jnp.dot(mixed_term, interpolation, precision=HIGH)
    flat_coupling = coupling.reshape(coupling.shape[0], coupling.shape[1] * coupling.shape[2])
    row_block = jnp.take(flat_coupling, ordering, axis=0).astype(jnp.float32)
    coupling_skel = row_block[:skeleton]
    coupling_red = row_block[skeleton:] - jnp.dot(interpolation.T, coupling_skel, precision=HIGH)
    factor = jnp.linalg.cholesky(bar_red_red)
    solved_skel = jax.scipy.linalg.solve_triangular(factor, bar_skel_red.T, lower=True)
    solved_far = jax.scipy.linalg.solve_triangular(factor, coupling_red, lower=True)
    own_block = skel_skel - jnp.dot(solved_skel.T, solved_skel, precision=HIGH)
    coupled = coupling_skel - jnp.dot(solved_skel.T, solved_far, precision=HIGH)
    slot_blocks = solved_far.reshape(solved_far.shape[0], coupling.shape[1], skeleton)
    updates = jnp.einsum('rki,rkj->kij', slot_blocks, slot_blocks, precision=HIGH)
    return (own_block, coupled, updates)

def reference(self_blocks, orders, interpolation, couplings, neighbours):
    boxes = PARENTS * 8
    own_blocks, coupled, updates = lax.map(eliminate, (self_blocks.reshape(boxes, BOXDOF, BOXDOF), orders.reshape(boxes, BOXDOF), interpolation.reshape(boxes, SKEL, RED), couplings.reshape(boxes, BOXDOF, NB, SKEL)))
    incoming = jax.ops.segment_sum(updates.reshape(boxes * NB, SKEL, SKEL), neighbours.reshape(boxes * NB), num_segments=boxes)
    skeleton_blocks = (own_blocks - incoming).reshape(PARENTS, 8, SKEL, SKEL)
    coupled = coupled.reshape(PARENTS, 8, SKEL, NB, SKEL)
    child_ids = jnp.arange(PARENTS, dtype=jnp.int32)[:, None, None, None] * 8 + jnp.arange(8, dtype=jnp.int32)[None, None, None, :]
    selector = (neighbours[:, :, :, None] == child_ids).astype(jnp.float32)
    off_blocks = jnp.einsum('pckd,pcikj->pcidj', selector, coupled, precision=HIGH)
    diag_blocks = jnp.einsum('pcij,cd->pcidj', skeleton_blocks, jnp.eye(8, dtype=jnp.float32), precision=HIGH)
    assembled = (off_blocks + diag_blocks).reshape(PARENTS, PDOF, PDOF)
    parent_matrix = 0.5 * (assembled + jnp.swapaxes(assembled, 1, 2))
    return (coupled.astype(jnp.bfloat16), parent_matrix)
```

```python
import jax
import jax.numpy as jnp
import numpy as np
from jax import lax
from jax.experimental import pallas as pl
from jax.experimental.pallas import tpu as pltpu
from jax.sharding import PartitionSpec as P

NSIB = 4
HIGH = lax.Precision.HIGHEST
F32 = jnp.float32
BF16 = jnp.bfloat16
NT = (((1,), (1,)), ((), ()))
NN = (((1,), (0,)), ((), ()))
TN = (((0,), (0,)), ((), ()))


def dot_high(a, b, dims=NN):
    return lax.dot_general(a, b, dims, precision=HIGH, preferred_element_type=F32)


def dot_bf16(a, b, dims=NN):
    return lax.dot_general(a, b, dims, preferred_element_type=F32)


def split2(x):
    hi = x.astype(BF16)
    return hi, (x - hi.astype(F32)).astype(BF16)


def split3(x):
    hi = x.astype(BF16)
    rest = x - hi.astype(F32)
    mid = rest.astype(BF16)
    return hi, mid, (rest - mid.astype(F32)).astype(BF16)


def dot3(a, b, dims=NN):
    ah, al = split2(a)
    bh, bl = split2(b)
    return dot_bf16(ah, bh, dims) + (dot_bf16(ah, bl, dims) + dot_bf16(al, bh, dims))


def iota(shape, dim):
    return lax.broadcasted_iota(jnp.int32, shape, dim)


def invert_cholesky(blocks):
    count = len(blocks)
    size = blocks[0].shape[0]
    groups = size // 8
    rows = [[block[8 * g : 8 * g + 8, :] for g in range(groups)] for block in blocks]
    lane = iota((8, size), 1)
    sub = iota((8, size), 0)
    pivots = [[None] * groups for _ in range(count)]
    for g in range(groups):
        found = [jnp.ones((8, size), F32) for _ in range(count)]
        for t in range(8):
            c = 8 * g + t
            at_lane = lane == c
            for b in range(count):
                pivot_rows = rows[b][g]
                column = jnp.broadcast_to(pivot_rows[:, c : c + 1], (8, size))
                pivot = jnp.broadcast_to(column[t : t + 1, :], (8, size))
                row = jnp.broadcast_to(pivot_rows[t : t + 1, :], (8, size))
                scaled = jnp.where(at_lane, 1.0, row) / pivot
                found[b] = jnp.where(sub == t, pivot, found[b])
                kept = jnp.where(at_lane, (sub == t).astype(F32), pivot_rows)
                rows[b][g] = kept - jnp.where(sub > t, column, 0.0) * scaled
                for i in range(g + 1, groups):
                    other = rows[b][i]
                    factor = jnp.broadcast_to(other[:, c : c + 1], (8, size))
                    rows[b][i] = jnp.where(at_lane, 0.0, other) - factor * scaled
        for b in range(count):
            pivots[b][g] = found[b]
    out = []
    for b in range(count):
        parts = [
            jnp.where(lane <= sub + 8 * g, rows[b][g] * lax.rsqrt(pivots[b][g]), 0.0)
            for g in range(groups)
        ]
        out.append(jnp.concatenate(parts, axis=0))
    return out


def factor_kernel(blocks_ref, orders_ref, interp_ref, high_ref, low_ref, own_ref, work, aug):
    count, dof, _ = blocks_ref.shape
    skel, red = interp_ref.shape[1:]
    for b in range(count):
        order = orders_ref[b]
        place_t = (iota((dof, dof), 0) == order).astype(F32).astype(BF16)
        column = jnp.broadcast_to(order.astype(F32), (128, dof)).T
        lanes = iota((dof, 128), 1).astype(F32)
        place = jnp.concatenate(
            [(column == lanes + 128.0 * q).astype(F32) for q in range(dof // 128)], axis=1
        )
        place_b = place.astype(BF16)
        parts = [dot_bf16(place_b, part).astype(BF16) for part in split3(blocks_ref[b])]
        ordered = dot_bf16(parts[0], place_t) + (
            dot_bf16(parts[1], place_t) + dot_bf16(parts[2], place_t)
        )
        a_ss = ordered[:skel, :skel]
        a_sr = ordered[:skel, skel:]
        interp = interp_ref[b]
        interp_t = interp.T
        bar_sr = a_sr - dot_high(a_ss, interp)
        left = jnp.concatenate([a_sr.T, interp_t], axis=1)
        right = jnp.concatenate([interp, bar_sr], axis=0)
        work[b] = ordered[skel:, skel:] - dot_high(left, right)
        pieces = [dot_bf16(part, place_b[:skel]) for part in split3(interp_t)]
        aug[b, :, :dof] = place[skel:] - (pieces[0] + (pieces[1] + pieces[2]))
        aug[b, :, dof:] = bar_sr.T
        own_ref[b] = a_ss
    panels = red // 128
    for k in range(panels):
        lo, hi = 128 * k, 128 * (k + 1)
        inverses = invert_cholesky([work[b, lo:hi, lo:hi] for b in range(count)])
        for b in range(count):
            solved = dot_high(inverses[b], aug[b, lo:hi, :])
            aug[b, lo:hi, :] = solved
            if hi < red:
                panel = dot_high(work[b, hi:, lo:hi], inverses[b], NT)
                work[b, hi:, hi:] = work[b, hi:, hi:] - dot_high(panel, panel, NT)
                aug[b, hi:, :] = aug[b, hi:, :] - dot_high(panel, solved)
    for b in range(count):
        solved_t = aug[b, :, dof:].T
        own_ref[b] = own_ref[b] - dot_high(solved_t, aug[b, :, dof:])
        grid_high, grid_low = split2(aug[b, :, :dof])
        high_ref[b, :red] = grid_high
        low_ref[b, :red] = grid_low
        column = jnp.broadcast_to(orders_ref[b].astype(F32), (128, dof)).T
        lanes = iota((skel, 128), 1).astype(F32)
        place_s = jnp.concatenate(
            [(column[:skel] == lanes + 128.0 * q).astype(F32) for q in range(dof // 128)], axis=1
        )
        last_high, last_low = split2(place_s - dot_high(solved_t, aug[b, :, :dof]))
        high_ref[b, red:] = last_high
        low_ref[b, red:] = last_low


def factor(self_blocks, orders, interpolation, interpret=False):
    count, dof, _ = self_blocks.shape
    skel, red = interpolation.shape[1:]
    return pl.pallas_call(
        factor_kernel,
        out_shape=(
            jax.ShapeDtypeStruct((count, dof, dof), BF16),
            jax.ShapeDtypeStruct((count, dof, dof), BF16),
            jax.ShapeDtypeStruct((count, skel, skel), F32),
        ),
        scratch_shapes=[pltpu.VMEM((count, red, red), F32), pltpu.VMEM((count, red, dof + skel), F32)],
        compiler_params=pltpu.CompilerParams(vmem_limit_bytes=60 << 20),
        cost_estimate=pl.CostEstimate(flops=8 << 30, bytes_accessed=6 << 20, transcendentals=0),
        interpret=interpret,
        name="factor",
    )(self_blocks, orders.reshape(count, 1, dof), interpolation)


def pack_symmetric(block, flag):
    half = block.shape[0] // 2
    top, bottom = block[:half], block[half:]
    lane, row = iota((half, 128), 1), iota((half, 128), 0)
    turned = pltpu.roll(bottom, half, 1)
    body = jnp.where((lane >= half) | (lane > row), top, turned)
    diagonal = jnp.sum(jnp.where(lane == row, top, 0.0), axis=0, keepdims=True)
    lanes = iota((8, 128), 1)
    tail = jnp.where(lanes < half, jnp.broadcast_to(diagonal, (8, 128)), flag)
    tail = jnp.where(iota((8, 128), 0) == 0, tail, 0.0)
    return jnp.concatenate([body, tail], axis=0)


def unpack_symmetric(packed):
    half = 64
    body = packed[:half]
    lane, row = iota((half, 128), 1), iota((half, 128), 0)
    upper = jnp.where((lane >= half) | (lane > row), body, 0.0)
    inner = jnp.where(lane < half, body, 0.0)
    lower = pltpu.roll(jnp.where(lane < row, inner, 0.0), half, 1)
    strict = jnp.concatenate([upper, lower], axis=0)
    first = jnp.where(lane == row, jnp.broadcast_to(packed[half : half + 1], (half, 128)), 0.0)
    second = pltpu.roll(jnp.where(lane == row, inner, 0.0), half, 1)
    return strict + strict.T + jnp.concatenate([first, second], axis=0)


def couple_kernel(
    place_ref, child_ref, high_ref, low_ref, w_ref, updated_ref, *rest
):
    far_count = len(rest) - 6
    far_outs, sib_outs = rest[:far_count], rest[far_count : far_count + 4]
    far, sib = rest[far_count + 4 :]
    box, step = pl.program_id(0), pl.program_id(1)
    red = high_ref.shape[1] - 128
    width = w_ref.shape[2] // 128

    @pl.when((box == 0) & (step == 0))
    def _():
        sib[...] = jnp.zeros_like(sib)

    w = w_ref[0]
    product = dot_bf16(high_ref[0], w) + dot_bf16(low_ref[0], w)
    coupled = product[red:]
    updated_ref[0] = coupled.astype(BF16)
    for s in range(width):
        part = slice(128 * s, 128 * (s + 1))
        zh, zl = split2(product[:red, part].T)
        cross = dot_bf16(zh, zl, NT)
        update = dot_bf16(zh, zh, NT) + (cross + cross.T)
        slot = step * width + s
        where = place_ref[box, slot]
        flag = child_ref[box, slot].astype(F32)
        packed = pack_symmetric(update, flag)

        @pl.when(step < NSIB // width)
        def _():
            sib[where, pl.ds(box * 128, 128), :] = coupled[:, part]
            sib[where, 256:328, :] = sib[where, 256:328, :] + packed

        @pl.when(step >= NSIB // width)
        def _():
            far[where] = packed

    @pl.when((box == pl.num_programs(0) - 1) & (step == pl.num_programs(1) - 1))
    def _():
        for i, out in enumerate(far_outs):
            out[...] = far[i]
        for i, out in enumerate(sib_outs):
            out[...] = sib[2 * i : 2 * i + 2]


def couple(place, child, high, low, w, far_count, interpret=False):
    count, dof, total = w.shape
    skel = dof - 384
    width = 2
    steps = total // (128 * width)
    whole = lambda shape: pl.BlockSpec(shape, lambda b, s, *_: (0,) * len(shape))
    return pl.pallas_call(
        couple_kernel,
        out_shape=(
            [jax.ShapeDtypeStruct((count, skel, total), BF16)]
            + [jax.ShapeDtypeStruct((72, 128), F32)] * far_count
            + [jax.ShapeDtypeStruct((2, 328, 128), F32)] * 4
        ),
        grid_spec=pltpu.PrefetchScalarGridSpec(
            num_scalar_prefetch=2,
            grid=(count, steps),
            in_specs=[
                pl.BlockSpec((1, dof, dof), lambda b, s, *_: (b, 0, 0)),
                pl.BlockSpec((1, dof, dof), lambda b, s, *_: (b, 0, 0)),
                pl.BlockSpec((1, dof, 128 * width), lambda b, s, *_: (b, 0, s)),
            ],
            out_specs=(
                [pl.BlockSpec((1, skel, 128 * width), lambda b, s, *_: (b, 0, s))]
                + [whole((72, 128))] * far_count
                + [whole((2, 328, 128))] * 4
            ),
            scratch_shapes=[pltpu.VMEM((far_count, 72, 128), F32), pltpu.VMEM((8, 328, 128), F32)],
        ),
        compiler_params=pltpu.CompilerParams(vmem_limit_bytes=40 << 20),
        cost_estimate=pl.CostEstimate(flops=6 << 30, bytes_accessed=8 << 20, transcendentals=0),
        interpret=interpret,
        name="couple",
    )(place, child, high, low, w)


def assemble_kernel(here_ref, own_ref, *rest):
    far_count = len(rest) - 8
    far = rest[:far_count]
    kept = rest[far_count : far_count + 4]
    got = rest[far_count + 4 : far_count + 7]
    out_ref = rest[-1]
    totals = [kept[0][c, 256:328, :] for c in range(2)]
    for block in far:
        packed = block[...]
        second = jnp.broadcast_to(packed[64:65, 64:65], packed.shape)
        totals = [totals[0] + packed * (1.0 - second), totals[1] + packed * second]
    for other in got:
        totals = [totals[c] + other[c, 256:328, :] for c in range(2)]
    skeleton = [own_ref[c] - unpack_symmetric(totals[c]) for c in range(2)]
    here = here_ref[0]
    wide = lambda ref: jnp.concatenate([ref[0, 0:256, :], ref[1, 0:256, :]], axis=1)
    zero = jnp.zeros((128, 128), F32)
    first = wide(kept[0]) + jnp.concatenate(
        [
            jnp.concatenate([skeleton[0], zero], axis=1),
            jnp.concatenate([zero, skeleton[1]], axis=1),
        ],
        axis=0,
    )
    out_ref[:, pl.ds(pl.multiple_of(here * 256, 256), 256)] = 0.5 * (first + first.T)
    for s in range(1, 4):
        column = (here + 4 - s) % 4
        block = 0.5 * (wide(kept[4 - s]) + wide(got[s - 1]).T)
        out_ref[:, pl.ds(pl.multiple_of(column * 256, 256), 256)] = block


def assemble(here, own, far, kept, got, interpret=False):
    vmem = pl.BlockSpec(memory_space=pltpu.VMEM)
    args = [own, *far, *kept, *got]
    return pl.pallas_call(
        assemble_kernel,
        out_shape=jax.ShapeDtypeStruct((256, 1024), F32),
        in_specs=[pl.BlockSpec(memory_space=pltpu.SMEM)] + [vmem] * len(args),
        out_specs=vmem,
        compiler_params=pltpu.CompilerParams(vmem_limit_bytes=40 << 20),
        interpret=interpret,
        name="assemble",
    )(here, *args)


def on_device(self_blocks, orders, interpolation, couplings, neighbours):
    boxes = lax.axis_size("box")
    sibs = lax.axis_size("sib")
    parent, sib = lax.axis_index("box"), lax.axis_index("sib")
    count, dof = orders.shape[1:]
    slots, skel = couplings.shape[3:]
    high, low, own = factor(self_blocks[0], orders[0], interpolation[0])
    reach = (slots - NSIB) * count // 2
    steps = [(j * (boxes // 2)) // reach for j in range(1, reach + 1)]
    steps += [boxes - (j * ((boxes - 1) // 2)) // reach for j in range(1, reach + 1)]
    rank = np.zeros((boxes,), np.int32)
    rank[steps] = np.arange(len(steps))
    ids = neighbours[0]
    far_place = jnp.asarray(rank)[(ids // 8 - parent) % boxes]
    sib_place = ((ids % 8) // count - sib) % sibs * count + ids % count
    place = jnp.where(jnp.arange(slots) < NSIB, sib_place, far_place).astype(jnp.int32)
    child = jnp.where(jnp.arange(slots) < NSIB, 0, ids % count).astype(jnp.int32)
    w = couplings.reshape(count, dof, slots * skel)
    updated, *rest = couple(place, child, high, low, w, len(steps))
    far, kept = rest[: len(steps)], rest[len(steps) :]
    got = [
        lax.ppermute(kept[s], "sib", [(i, (i + s) % sibs) for i in range(sibs)])
        for s in range(1, sibs)
    ]
    far = [
        lax.ppermute(block, "box", [(i, (i + step) % boxes) for i in range(boxes)])
        for block, step in zip(far, steps)
    ]
    rows = assemble(sib.reshape(1).astype(jnp.int32), own, far, kept, got)
    return updated.reshape(1, count, skel, slots, skel), rows[None]


def solution(mesh):
    return jax.shard_map(
        on_device,
        mesh=mesh,
        in_specs=(
            P("box", "sib", None, None),
            P("box", "sib", None),
            P("box", "sib", None, None),
            P("box", "sib", None, None, None),
            P("box", "sib", None),
        ),
        out_specs=(P("box", "sib", None, None, None), P("box", "sib", None)),
        check_vma=False,
    )
```

```python
import functools
import jax
import jax.numpy as jnp
import numpy as np
from jax import lax
from jax.experimental import pallas as pl
from jax.experimental.pallas import tpu as pltpu
from jax.sharding import PartitionSpec as P

NSIB = 4
HIGH = lax.Precision.HIGHEST
F32 = jnp.float32
BF16 = jnp.bfloat16
NT = (((1,), (1,)), ((), ()))
NN = (((1,), (0,)), ((), ()))
TN = (((0,), (0,)), ((), ()))


def dot_high(a, b, dims=NN):
    return lax.dot_general(a, b, dims, precision=HIGH, preferred_element_type=F32)


def dot_bf16(a, b, dims=NN):
    return lax.dot_general(a, b, dims, preferred_element_type=F32)


def split2(x):
    hi = x.astype(BF16)
    return hi, (x - hi.astype(F32)).astype(BF16)


def split3(x):
    hi = x.astype(BF16)
    rest = x - hi.astype(F32)
    mid = rest.astype(BF16)
    return hi, mid, (rest - mid.astype(F32)).astype(BF16)


def dot3(a, b, dims=NN):
    ah, al = split2(a)
    bh, bl = split2(b)
    return dot_bf16(ah, bh, dims) + (dot_bf16(ah, bl, dims) + dot_bf16(al, bh, dims))


def iota(shape, dim):
    return lax.broadcasted_iota(jnp.int32, shape, dim)


def spread(x, lane):
    return jnp.take_along_axis(x, jnp.full(x.shape, lane, jnp.int32), axis=1)


def eliminate_rows(panels, base):
    shape = panels[0].shape
    lane, sub = iota(shape, 1), iota(shape, 0)
    panels = list(panels)
    columns = [[spread(panel, base + t) for t in range(8)] for panel in panels]
    inverses = [jnp.ones(shape, F32) for _ in panels]
    for t in range(8):
        here = lane == base + t
        one = (sub == t).astype(F32)
        for b, panel in enumerate(panels):
            column = columns[b][t]
            inverse = 1.0 / jnp.broadcast_to(column[t : t + 1, :], shape)
            inverses[b] = jnp.where(sub == t, inverse, inverses[b])
            ratio = jnp.where(sub > t, column, 0.0) * inverse
            for u in range(t + 1, 8):
                later = columns[b][u]
                columns[b][u] = later - ratio * jnp.broadcast_to(later[t : t + 1, :], shape)
            row = jnp.where(here, 1.0, jnp.broadcast_to(panel[t : t + 1, :], shape))
            panels[b] = jnp.where(here, one, panel) - ratio * row
    return panels, inverses


def invert_cholesky(blocks):
    count, size, span = len(blocks), blocks[0].shape[0], 32
    lane, sub = iota((8, size), 1), iota((8, size), 0)
    rows = [[block[8 * g : 8 * g + 8, :] for g in range(size // 8)] for block in blocks]
    out = [[] for _ in blocks]
    for start in range(0, size, span):
        end = start + span
        finals, scaled_rows = [[] for _ in blocks], [[] for _ in blocks]
        for g in range(start // 8, end // 8):
            base = 8 * g
            panels, inverses = eliminate_rows([rows[b][g] for b in range(count)], base)
            for b in range(count):
                panel = panels[b]
                scaled = panel * inverses[b]
                beyond = lane > sub + base
                out[b].append(jnp.where(beyond, 0.0, panel * jnp.sqrt(inverses[b])))
                finals[b].append(panel)
                scaled_rows[b].append(jnp.where(beyond & (lane < end), 0.0, scaled))
                if base + 8 == end:
                    continue
                scaled = jnp.where(beyond & (lane < base + 8), 0.0, scaled)
                flipped = panel.T
                clear = (lane >= base) & (lane < base + 8)
                for i in range(g + 1, end // 8):
                    factors = flipped[8 * i : 8 * i + 8, :]
                    terms = [
                        jnp.broadcast_to(factors[:, t : t + 1], (8, size))
                        * jnp.broadcast_to(scaled[t : t + 1, :], (8, size))
                        for t in range(8)
                    ]
                    while len(terms) > 1:
                        terms = [terms[j] + terms[j + 1] for j in range(0, len(terms), 2)]
                    rows[b][i] = jnp.where(clear, 0.0, rows[b][i]) - terms[0]
        if end < size:
            clear = (lane >= start) & (lane < end)
            for b in range(count):
                factors = jnp.concatenate(finals[b], axis=0).T[end:]
                update = dot_high(factors, jnp.concatenate(scaled_rows[b], axis=0))
                for i in range(end // 8, size // 8):
                    k = 8 * i - end
                    rows[b][i] = jnp.where(clear, 0.0, rows[b][i]) - update[k : k + 8]
    return [jnp.concatenate(parts, axis=0) for parts in out]


def factor_kernel(blocks_ref, orders_ref, interp_ref, high_ref, low_ref, own_ref, work, aug):
    count, dof, _ = blocks_ref.shape
    skel, red = interp_ref.shape[1:]
    for b in range(count):
        order = orders_ref[b]
        place_t = (iota((dof, dof), 0) == order).astype(F32).astype(BF16)
        column = jnp.broadcast_to(order.astype(F32), (128, dof)).T
        lanes = iota((dof, 128), 1).astype(F32)
        place = jnp.concatenate(
            [(column == lanes + 128.0 * q).astype(F32) for q in range(dof // 128)], axis=1
        )
        place_b = place.astype(BF16)
        parts = [dot_bf16(place_b, part).astype(BF16) for part in split3(blocks_ref[b])]
        ordered = dot_bf16(parts[0], place_t) + (
            dot_bf16(parts[1], place_t) + dot_bf16(parts[2], place_t)
        )
        a_ss = ordered[:skel, :skel]
        a_sr = ordered[:skel, skel:]
        interp = interp_ref[b]
        interp_t = interp.T
        bar_sr = a_sr - dot_high(a_ss, interp)
        left = jnp.concatenate([a_sr.T, interp_t], axis=1)
        right = jnp.concatenate([interp, bar_sr], axis=0)
        work[b] = ordered[skel:, skel:] - dot_high(left, right)
        pieces = [dot_bf16(part, place_b[:skel]) for part in split3(interp_t)]
        aug[b, :, :dof] = place[skel:] - (pieces[0] + (pieces[1] + pieces[2]))
        aug[b, :, dof:] = bar_sr.T
        own_ref[b] = a_ss
    panels = red // 128
    for k in range(panels):
        lo, hi = 128 * k, 128 * (k + 1)
        inverses = invert_cholesky([work[b, lo:hi, lo:hi] for b in range(count)])
        for b in range(count):
            solved = dot_high(inverses[b], aug[b, lo:hi, :])
            aug[b, lo:hi, :] = solved
            if hi < red:
                panel = dot_high(work[b, hi:, lo:hi], inverses[b], NT)
                work[b, hi:, hi:] = work[b, hi:, hi:] - dot_high(panel, panel, NT)
                aug[b, hi:, :] = aug[b, hi:, :] - dot_high(panel, solved)
    for b in range(count):
        solved_t = aug[b, :, dof:].T
        own_ref[b] = own_ref[b] - dot_high(solved_t, aug[b, :, dof:])
        grid_high, grid_low = split2(aug[b, :, :dof])
        high_ref[b, :red] = grid_high
        low_ref[b, :red] = grid_low
        column = jnp.broadcast_to(orders_ref[b].astype(F32), (128, dof)).T
        lanes = iota((skel, 128), 1).astype(F32)
        place_s = jnp.concatenate(
            [(column[:skel] == lanes + 128.0 * q).astype(F32) for q in range(dof // 128)], axis=1
        )
        last_high, last_low = split2(place_s - dot_high(solved_t, aug[b, :, :dof]))
        high_ref[b, red:] = last_high
        low_ref[b, red:] = last_low


def factor(self_blocks, orders, interpolation, interpret=False):
    count, dof, _ = self_blocks.shape
    skel, red = interpolation.shape[1:]
    return pl.pallas_call(
        factor_kernel,
        out_shape=(
            jax.ShapeDtypeStruct((count, dof, dof), BF16),
            jax.ShapeDtypeStruct((count, dof, dof), BF16),
            jax.ShapeDtypeStruct((count, skel, skel), F32),
        ),
        scratch_shapes=[pltpu.VMEM((count, red, red), F32), pltpu.VMEM((count, red, dof + skel), F32)],
        compiler_params=pltpu.CompilerParams(vmem_limit_bytes=24 << 20),
        cost_estimate=pl.CostEstimate(flops=8 << 30, bytes_accessed=6 << 20, transcendentals=0),
        interpret=interpret,
        name="factor",
    )(self_blocks, orders.reshape(count, 1, dof), interpolation)


def pack_symmetric(block, flag):
    half = block.shape[0] // 2
    top, bottom = block[:half], block[half:]
    lane, row = iota((half, 128), 1), iota((half, 128), 0)
    turned = pltpu.roll(bottom, half, 1)
    body = jnp.where((lane >= half) | (lane > row), top, turned)
    diagonal = jnp.sum(jnp.where(lane == row, top, 0.0), axis=0, keepdims=True)
    return body, jnp.where(iota((1, 128), 1) < half, diagonal, flag)


def unpack_symmetric(body, tail):
    half = 64
    lane, row = iota((half, 128), 1), iota((half, 128), 0)
    upper = jnp.where((lane >= half) | (lane > row), body, 0.0)
    inner = jnp.where(lane < half, body, 0.0)
    lower = pltpu.roll(jnp.where(lane < row, inner, 0.0), half, 1)
    strict = jnp.concatenate([upper, lower], axis=0)
    first = jnp.where(lane == row, jnp.broadcast_to(tail, (half, 128)), 0.0)
    second = pltpu.roll(jnp.where(lane == row, inner, 0.0), half, 1)
    return strict + strict.T + jnp.concatenate([first, second], axis=0)


Y, Z, C = 4, 8, 2
STAGES = [(dy, dc) for dy in range(Y) for dc in range(C)]
TABLE = 128


def place_of(box):
    return box // (Z * C), box // C % Z, box % C


def box_of(y, z, c):
    return (y % Y * Z + z % Z) * C + c % C


def plan(boxes, reach):
    steps = [(j * (boxes // 2)) // reach for j in range(1, reach + 1)]
    steps += [boxes - (j * ((boxes - 1) // 2)) // reach for j in range(1, reach + 1)]
    lists = []
    for box in range(boxes):
        y, z, c = place_of(box)
        by_stage = {stage: [] for stage in STAGES}
        for step in steps:
            ty, tz, tc = place_of((box + step) % boxes)
            by_stage[(ty - y) % Y, (tc - c) % C].append((step, (tz - z) % Z))
        lists.append(by_stage)
    caps = [max(len(found[stage]) for found in lists) for stage in STAGES]
    starts = np.concatenate([[0], np.cumsum(caps)]).tolist()
    table = np.zeros((boxes, TABLE), np.int32)
    for box in range(boxes):
        y, z, c = place_of(box)
        for s, stage in enumerate(STAGES):
            for j, (step, _) in enumerate(lists[box][stage]):
                table[box, step] = starts[s] + j
            source = lists[box_of(y - stage[0], z, c - stage[1])]
            for j, (_, shift) in enumerate(source[stage]):
                table[box, boxes + starts[s] + j] = shift
    return table, caps, starts


def couple_kernel(
    ids_ref, table_ref, where_ref, high_ref, low_ref, w_ref, updated_ref, *rest, caps, starts, boxes
):
    far_outs, sib_outs = rest[: len(caps)], rest[len(caps) : len(caps) + 4]
    by_slot, coupled_slots, bodies, tails, sib = rest[len(caps) + 4 :]
    box = pl.program_id(0)
    red = high_ref.shape[1] - 128
    slots = by_slot.shape[0]
    parent, this_sib = where_ref[0], where_ref[1]

    @pl.when(box == 0)
    def _():
        sib[...] = jnp.zeros_like(sib)
        bodies[...] = jnp.zeros_like(bodies)
        tails[...] = jnp.zeros_like(tails)

    by_slot[...] = jnp.swapaxes(w_ref[0], 0, 1)

    def four(first, far):
        for pair in (0, 2):
            w = jnp.concatenate([by_slot[first + pair], by_slot[first + pair + 1]], axis=1)
            product = dot_bf16(high_ref[0], w) + dot_bf16(low_ref[0], w)
            for s in range(2):
                slot = first + pair + s
                part = slice(128 * s, 128 * (s + 1))
                coupled = product[red:, part]
                coupled_slots[slot] = coupled.astype(BF16)
                zh, zl = split2(product[:red, part].T)
                cross = dot_bf16(zh, zl, NT)
                update = dot_bf16(zh, zh, NT) + (cross + cross.T)
                other = ids_ref[box, slot]
                child = other & 1
                body, tail = pack_symmetric(update, child.astype(F32))
                if far:
                    place = table_ref[0, ((other >> 3) - parent) & (boxes - 1)]
                    bodies[place] = body
                    tails[pl.ds(place, 1), :] = tail
                else:
                    place = ((((other >> 1) & 3) - this_sib) & 3) * 2 + child
                    sib[place, pl.ds(pl.multiple_of(box * 128, 128), 128), :] = coupled
                    sib[place, 256:320, :] = sib[place, 256:320, :] + body
                    sib[place, 320:321, :] = sib[place, 320:321, :] + tail

    four(0, False)

    @pl.loop(1, slots // 4)
    def _(group):
        four(group * 4, True)

    updated_ref[0] = jnp.swapaxes(coupled_slots[...], 0, 1)

    @pl.when(box == pl.num_programs(0) - 1)
    def _():
        for s, out in enumerate(far_outs):
            for j in range(caps[s]):
                out[64 * j : 64 * j + 64] = bodies[starts[s] + j]
            out[64 * caps[s] : 64 * caps[s] + 8] = jnp.concatenate(
                [tails[starts[s] : starts[s] + caps[s]], jnp.zeros((8 - caps[s], 128), F32)], axis=0
            )
        for i, out in enumerate(sib_outs):
            out[...] = sib[2 * i : 2 * i + 2]


def couple(ids, table, where, high, low, w, caps, starts, boxes, interpret=False):
    count, dof, slots, skel = w.shape
    whole = lambda shape: pl.BlockSpec(shape, lambda b, *_: (0,) * len(shape))
    by_box = lambda shape: pl.BlockSpec((1,) + shape, lambda b, *_: (b,) + (0,) * len(shape))
    outs = [(64 * cap + 8, 128) for cap in caps] + [(2, 328, 128)] * 4
    return pl.pallas_call(
        functools.partial(couple_kernel, caps=caps, starts=starts, boxes=boxes),
        out_shape=(
            [jax.ShapeDtypeStruct((count, skel, slots, skel), BF16)]
            + [jax.ShapeDtypeStruct(shape, F32) for shape in outs]
        ),
        grid_spec=pltpu.PrefetchScalarGridSpec(
            num_scalar_prefetch=3,
            grid=(count,),
            in_specs=[by_box((dof, dof)), by_box((dof, dof)), by_box((dof, slots, skel))],
            out_specs=[by_box((skel, slots, skel))] + [whole(shape) for shape in outs],
            scratch_shapes=[
                pltpu.VMEM((slots, dof, skel), BF16),
                pltpu.VMEM((slots, skel, skel), BF16),
                pltpu.VMEM((starts[-1], 64, 128), F32),
                pltpu.VMEM((-(-starts[-1] // 8) * 8, 128), F32),
                pltpu.VMEM((8, 328, 128), F32),
            ],
        ),
        compiler_params=pltpu.CompilerParams(vmem_limit_bytes=32 << 20),
        cost_estimate=pl.CostEstimate(flops=6 << 30, bytes_accessed=8 << 20, transcendentals=0),
        interpret=interpret,
        name="couple",
    )(ids, table, where, high, low, w)


def route_kernel(table_ref, *rest, caps, starts, boxes):
    got, outs, sums = rest[: len(caps)], rest[len(caps) : -1], rest[-1]
    sums[...] = jnp.zeros_like(sums)
    for s, block in enumerate(got):
        for j in range(caps[s]):
            shift = table_ref[0, boxes + starts[s] + j]
            body = block[64 * j : 64 * j + 64]
            tail = block[64 * caps[s] + j : 64 * caps[s] + j + 1]
            second = tail[:, 64:65]
            share = jnp.broadcast_to(second, body.shape)
            row_share = jnp.broadcast_to(second, tail.shape)
            sums[shift, 0:64] = sums[shift, 0:64] + body * (1.0 - share)
            sums[shift, 64:128] = sums[shift, 64:128] + body * share
            sums[shift, 128:129] = sums[shift, 128:129] + tail * (1.0 - row_share)
            sums[shift, 129:130] = sums[shift, 129:130] + tail * row_share
    for i, out in enumerate(outs):
        out[...] = sums[i]


def route(table, got, caps, starts, boxes, interpret=False):
    vmem = pl.BlockSpec(memory_space=pltpu.VMEM)
    return pl.pallas_call(
        functools.partial(route_kernel, caps=caps, starts=starts, boxes=boxes),
        out_shape=[jax.ShapeDtypeStruct((136, 128), F32)] * Z,
        in_specs=[pl.BlockSpec(memory_space=pltpu.SMEM)] + [vmem] * len(got),
        out_specs=[vmem] * Z,
        scratch_shapes=[pltpu.VMEM((Z, 136, 128), F32)],
        compiler_params=pltpu.CompilerParams(vmem_limit_bytes=16 << 20),
        cost_estimate=pl.CostEstimate(flops=1 << 22, bytes_accessed=2 << 20, transcendentals=0),
        interpret=interpret,
        name="route",
    )(table, *got)


def assemble_kernel(where_ref, own_ref, *rest):
    far = rest[:-8]
    kept = rest[-8:-4]
    got = rest[-4:-1]
    out_ref = rest[-1]
    sibs = [kept[0]] + list(got)
    skeleton = []
    for c in range(2):
        body = sum(block[64 * c : 64 * c + 64] for block in far)
        tail = sum(block[128 + c : 129 + c] for block in far)
        for other in sibs:
            body = body + other[c, 256:320, :]
            tail = tail + other[c, 320:321, :]
        skeleton.append(own_ref[c] - unpack_symmetric(body, tail))
    here = where_ref[1]
    wide = lambda ref: jnp.concatenate([ref[0, 0:256, :], ref[1, 0:256, :]], axis=1)
    zero = jnp.zeros((128, 128), F32)
    first = wide(kept[0]) + jnp.concatenate(
        [
            jnp.concatenate([skeleton[0], zero], axis=1),
            jnp.concatenate([zero, skeleton[1]], axis=1),
        ],
        axis=0,
    )
    out_ref[:, pl.ds(pl.multiple_of(here * 256, 256), 256)] = 0.5 * (first + first.T)
    for s in range(1, 4):
        column = (here + 4 - s) & 3
        block = 0.5 * (wide(kept[4 - s]) + wide(got[s - 1]).T)
        out_ref[:, pl.ds(pl.multiple_of(column * 256, 256), 256)] = block


def assemble(where, own, far, kept, got, interpret=False):
    vmem = pl.BlockSpec(memory_space=pltpu.VMEM)
    args = [own, *far, *kept, *got]
    return pl.pallas_call(
        assemble_kernel,
        out_shape=jax.ShapeDtypeStruct((256, 1024), F32),
        in_specs=[pl.BlockSpec(memory_space=pltpu.SMEM)] + [vmem] * len(args),
        out_specs=vmem,
        compiler_params=pltpu.CompilerParams(vmem_limit_bytes=24 << 20),
        interpret=interpret,
        name="assemble",
    )(where, *args)


def on_device(self_blocks, orders, interpolation, couplings, neighbours):
    boxes = lax.axis_size("box")
    sibs = lax.axis_size("sib")
    parent, sib = lax.axis_index("box"), lax.axis_index("sib")
    count = orders.shape[1]
    slots = couplings.shape[3]
    where = jnp.stack([parent, sib]).astype(jnp.int32)
    plans, caps, starts = plan(boxes, (slots - NSIB) * count // 2)
    table = lax.dynamic_slice(jnp.asarray(plans), (parent, 0), (1, TABLE))
    high, low, own = factor(self_blocks[0], orders[0], interpolation[0])
    updated, *rest = couple(
        neighbours[0], table, where, high, low, couplings[0], caps, starts, boxes
    )
    sent, kept = rest[: len(caps)], rest[len(caps) :]
    got = [sent[0]]
    for s in range(1, len(STAGES)):
        dy, dc = STAGES[s]
        moves = []
        for i in range(boxes):
            y, z, c = place_of(i)
            moves.append((i, box_of(y + dy, z, c + dc)))
        got.append(lax.ppermute(sent[s], "box", moves))
    sib_got = [
        lax.ppermute(kept[s], "sib", [(i, (i + s) % sibs) for i in range(sibs)])
        for s in range(1, sibs)
    ]
    sums = route(table, got, caps, starts, boxes)
    far = [sums[0]]
    for dz in (4, 3, 5, 2, 6, 1, 7):
        moves = []
        for i in range(boxes):
            y, z, c = place_of(i)
            moves.append((i, box_of(y, z + dz, c)))
        far.append(lax.ppermute(sums[dz], "box", moves))
    rows = assemble(where, own, far, kept, sib_got)
    return updated[None], rows[None]


def solution(mesh):
    return jax.shard_map(
        on_device,
        mesh=mesh,
        in_specs=(
            P("box", "sib", None, None),
            P("box", "sib", None),
            P("box", "sib", None, None),
            P("box", "sib", None, None, None),
            P("box", "sib", None),
        ),
        out_specs=(P("box", "sib", None, None, None), P("box", "sib", None)),
        check_vma=False,
    )
```

```python
import functools
import jax
import jax.numpy as jnp
import numpy as np
from jax import lax
from jax.experimental import pallas as pl
from jax.experimental.pallas import tpu as pltpu
from jax.sharding import PartitionSpec as P


NSIB = 4
HIGH = lax.Precision.HIGHEST
F32 = jnp.float32
BF16 = jnp.bfloat16
NT = (((1,), (1,)), ((), ()))
NN = (((1,), (0,)), ((), ()))


def dot_high(a, b, dims=NN):
    return lax.dot_general(a, b, dims, precision=HIGH, preferred_element_type=F32)


def dot_bf16(a, b, dims=NN):
    return lax.dot_general(a, b, dims, preferred_element_type=F32)


def split2(x):
    hi = x.astype(BF16)
    return hi, (x - hi.astype(F32)).astype(BF16)


def split3(x):
    hi = x.astype(BF16)
    rest = x - hi.astype(F32)
    mid = rest.astype(BF16)
    return hi, mid, (rest - mid.astype(F32)).astype(BF16)


def iota(shape, dim):
    return lax.broadcasted_iota(jnp.int32, shape, dim)


def spread(x, lane):
    return jnp.take_along_axis(x, jnp.full(x.shape, lane, jnp.int32), axis=1)


def eliminate_rows(panels, base):
    shape = panels[0].shape
    lane, sub = iota(shape, 1), iota(shape, 0)
    panels = list(panels)
    columns = [[spread(panel, base + t) for t in range(8)] for panel in panels]
    inverses = [jnp.ones(shape, F32) for _ in panels]
    for t in range(8):
        here = lane == base + t
        one = (sub == t).astype(F32)
        for b, panel in enumerate(panels):
            column = columns[b][t]
            inverse = 1.0 / jnp.broadcast_to(column[t : t + 1, :], shape)
            inverses[b] = jnp.where(sub == t, inverse, inverses[b])
            ratio = jnp.where(sub > t, column, 0.0) * inverse
            for u in range(t + 1, 8):
                later = columns[b][u]
                columns[b][u] = later - ratio * jnp.broadcast_to(later[t : t + 1, :], shape)
            row = jnp.where(here, 1.0, jnp.broadcast_to(panel[t : t + 1, :], shape))
            panels[b] = jnp.where(here, one, panel) - ratio * row
    return panels, inverses


def invert_cholesky(blocks):
    count, size, span = len(blocks), blocks[0].shape[0], 32
    lane, sub = iota((8, size), 1), iota((8, size), 0)
    rows = [[block[8 * g : 8 * g + 8, :] for g in range(size // 8)] for block in blocks]
    out = [[] for _ in blocks]
    for start in range(0, size, span):
        end = start + span
        finals, scaled_rows = [[] for _ in blocks], [[] for _ in blocks]
        for g in range(start // 8, end // 8):
            base = 8 * g
            panels, inverses = eliminate_rows([rows[b][g] for b in range(count)], base)
            for b in range(count):
                panel = panels[b]
                scaled = panel * inverses[b]
                beyond = lane > sub + base
                out[b].append(jnp.where(beyond, 0.0, panel * jnp.sqrt(inverses[b])))
                finals[b].append(panel)
                scaled_rows[b].append(jnp.where(beyond & (lane < end), 0.0, scaled))
                if base + 8 == end:
                    continue
                scaled = jnp.where(beyond & (lane < base + 8), 0.0, scaled)
                flipped = panel.T
                clear = (lane >= base) & (lane < base + 8)
                for i in range(g + 1, end // 8):
                    factors = flipped[8 * i : 8 * i + 8, :]
                    terms = [
                        jnp.broadcast_to(factors[:, t : t + 1], (8, size))
                        * jnp.broadcast_to(scaled[t : t + 1, :], (8, size))
                        for t in range(8)
                    ]
                    while len(terms) > 1:
                        terms = [terms[j] + terms[j + 1] for j in range(0, len(terms), 2)]
                    rows[b][i] = jnp.where(clear, 0.0, rows[b][i]) - terms[0]
        if end < size:
            clear = (lane >= start) & (lane < end)
            for b in range(count):
                factors = jnp.concatenate(finals[b], axis=0).T[end:]
                update = dot_high(factors, jnp.concatenate(scaled_rows[b], axis=0))
                for i in range(end // 8, size // 8):
                    k = 8 * i - end
                    rows[b][i] = jnp.where(clear, 0.0, rows[b][i]) - update[k : k + 8]
    return [jnp.concatenate(parts, axis=0) for parts in out]


def factor_kernel(blocks_ref, orders_ref, interp_ref, high_ref, low_ref, own_ref, work, aug):
    count, dof, _ = blocks_ref.shape
    skel, red = interp_ref.shape[1:]
    for b in range(count):
        order = orders_ref[b : b + 1, :]
        place_t = (iota((dof, dof), 0) == order).astype(F32).astype(BF16)
        column = jnp.broadcast_to(order.astype(F32), (128, dof)).T
        lanes = iota((dof, 128), 1).astype(F32)
        place = jnp.concatenate(
            [(column == lanes + 128.0 * q).astype(F32) for q in range(dof // 128)], axis=1
        )
        place_b = place.astype(BF16)
        parts = [dot_bf16(place_b, part).astype(BF16) for part in split3(blocks_ref[b])]
        ordered = dot_bf16(parts[0], place_t) + (
            dot_bf16(parts[1], place_t) + dot_bf16(parts[2], place_t)
        )
        a_ss = ordered[:skel, :skel]
        a_sr = ordered[:skel, skel:]
        interp = interp_ref[b]
        interp_t = interp.T
        bar_sr = a_sr - dot_high(a_ss, interp)
        left = jnp.concatenate([a_sr.T, interp_t], axis=1)
        right = jnp.concatenate([interp, bar_sr], axis=0)
        work[b] = ordered[skel:, skel:] - dot_high(left, right)
        pieces = [dot_bf16(part, place_b[:skel]) for part in split3(interp_t)]
        aug[b, :, :dof] = place[skel:] - (pieces[0] + (pieces[1] + pieces[2]))
        aug[b, :, dof:] = bar_sr.T
        own_ref[b] = a_ss
    panels = red // 128
    for k in range(panels):
        lo, hi = 128 * k, 128 * (k + 1)
        inverses = invert_cholesky([work[b, lo:hi, lo:hi] for b in range(count)])
        for b in range(count):
            solved = dot_high(inverses[b], aug[b, lo:hi, :])
            aug[b, lo:hi, :] = solved
            if hi < red:
                panel = dot_high(work[b, hi:, lo:hi], inverses[b], NT)
                work[b, hi:, hi:] = work[b, hi:, hi:] - dot_high(panel, panel, NT)
                aug[b, hi:, :] = aug[b, hi:, :] - dot_high(panel, solved)
    for b in range(count):
        solved_t = aug[b, :, dof:].T
        own_ref[b] = own_ref[b] - dot_high(solved_t, aug[b, :, dof:])
        grid_high, grid_low = split2(aug[b, :, :dof])
        high_ref[b, :red] = grid_high
        low_ref[b, :red] = grid_low
        column = jnp.broadcast_to(orders_ref[b : b + 1, :].astype(F32), (128, dof)).T
        lanes = iota((skel, 128), 1).astype(F32)
        place_s = jnp.concatenate(
            [(column[:skel] == lanes + 128.0 * q).astype(F32) for q in range(dof // 128)], axis=1
        )
        last_high, last_low = split2(place_s - dot_high(solved_t, aug[b, :, :dof]))
        high_ref[b, red:] = last_high
        low_ref[b, red:] = last_low


def factor(self_blocks, orders, interpolation, interpret=False):
    count, dof, _ = self_blocks.shape
    skel, red = interpolation.shape[1:]
    return pl.pallas_call(
        factor_kernel,
        out_shape=(
            jax.ShapeDtypeStruct((count, dof, dof), BF16),
            jax.ShapeDtypeStruct((count, dof, dof), BF16),
            jax.ShapeDtypeStruct((count, skel, skel), F32),
        ),
        scratch_shapes=[pltpu.VMEM((count, red, red), F32), pltpu.VMEM((count, red, dof + skel), F32)],
        compiler_params=pltpu.CompilerParams(vmem_limit_bytes=24 << 20),
        cost_estimate=pl.CostEstimate(flops=8 << 30, bytes_accessed=6 << 20, transcendentals=0),
        interpret=interpret,
        name="factor",
    )(self_blocks, orders, interpolation)


def pack_symmetric(block, flag):
    half = block.shape[0] // 2
    top, bottom = block[:half], block[half:]
    lane, row = iota((half, 128), 1), iota((half, 128), 0)
    turned = pltpu.roll(bottom, half, 1)
    body = jnp.where((lane >= half) | (lane > row), top, turned)
    diagonal = jnp.sum(jnp.where(lane == row, top, 0.0), axis=0, keepdims=True)
    return body, jnp.where(iota((1, 128), 1) < half, diagonal, flag)


def unpack_symmetric(body, tail):
    half = 64
    lane, row = iota((half, 128), 1), iota((half, 128), 0)
    upper = jnp.where((lane >= half) | (lane > row), body, 0.0)
    inner = jnp.where(lane < half, body, 0.0)
    lower = pltpu.roll(jnp.where(lane < row, inner, 0.0), half, 1)
    strict = jnp.concatenate([upper, lower], axis=0)
    first = jnp.where(lane == row, jnp.broadcast_to(tail, (half, 128)), 0.0)
    second = pltpu.roll(jnp.where(lane == row, inner, 0.0), half, 1)
    return strict + strict.T + jnp.concatenate([first, second], axis=0)


Y, Z, C = 4, 8, 2
STAGES = [(dy, dc) for dy in range(Y) for dc in range(C)]
TABLE = 128


def place_of(box):
    return box // (Z * C), box // C % Z, box % C


def box_of(y, z, c):
    return (y % Y * Z + z % Z) * C + c % C


def plan(boxes, reach):
    steps = [(j * (boxes // 2)) // reach for j in range(1, reach + 1)]
    steps += [boxes - (j * ((boxes - 1) // 2)) // reach for j in range(1, reach + 1)]
    lists = []
    for box in range(boxes):
        y, z, c = place_of(box)
        by_stage = {stage: [] for stage in STAGES}
        for step in steps:
            ty, tz, tc = place_of((box + step) % boxes)
            by_stage[(ty - y) % Y, (tc - c) % C].append((step, (tz - z) % Z))
        lists.append(by_stage)
    caps = [max(len(found[stage]) for found in lists) for stage in STAGES]
    starts = np.concatenate([[0], np.cumsum(caps)]).tolist()
    table = np.zeros((boxes, TABLE), np.int32)
    for box in range(boxes):
        y, z, c = place_of(box)
        for s, stage in enumerate(STAGES):
            for j, (step, _) in enumerate(lists[box][stage]):
                table[box, step] = starts[s] + j
            source = lists[box_of(y - stage[0], z, c - stage[1])]
            for j, (_, shift) in enumerate(source[stage]):
                table[box, boxes + starts[s] + j] = shift
    return table, caps, starts


def row_spec(table):
    return pl.BlockSpec(
        (8, table.shape[1]), lambda *args: (args[-1][0] // 8, 0), memory_space=pltpu.SMEM
    )


def gram(z_t):
    high, low = split2(z_t)
    return dot_bf16(high, high, NT) + (dot_bf16(high, low, NT) + dot_bf16(low, high, NT))


def slot_updates(high_ref, low_ref, slot_pair):
    product = dot_bf16(high_ref[0], slot_pair) + dot_bf16(low_ref[0], slot_pair)
    both = gram(product.T)
    return both[:128, :128], both[128:, 128:]


def far_kernel(ids_ref, where_ref, table_ref, high_ref, low_ref, w_ref, *rest, caps, starts, boxes):
    outs, (bodies, tails) = rest[: len(caps)], rest[len(caps) :]
    box = pl.program_id(0)
    parent = where_ref[0]

    @pl.when(box == 0)
    def _():
        bodies[...] = jnp.zeros_like(bodies)
        tails[...] = jnp.zeros_like(tails)

    slots = w_ref.shape[2]
    by_slot = jnp.swapaxes(w_ref[0], 0, 1)
    for first in range(NSIB, slots, 2):
        pair = jnp.concatenate([by_slot[first], by_slot[first + 1]], axis=1)
        for s, update in enumerate(slot_updates(high_ref, low_ref, pair)):
            other = ids_ref[box, first + s]
            body, tail = pack_symmetric(update, (other & 1).astype(F32))
            place = table_ref[parent & 7, ((other >> 3) - parent) & (boxes - 1)]
            bodies[place] = body
            tails[pl.ds(place, 1), :] = tail

    @pl.when(box == pl.num_programs(0) - 1)
    def _():
        for s, out in enumerate(outs):
            for j in range(caps[s]):
                out[64 * j : 64 * j + 64] = bodies[starts[s] + j]
            out[64 * caps[s] : 64 * caps[s] + 8] = jnp.concatenate(
                [tails[starts[s] : starts[s] + caps[s]], jnp.zeros((8 - caps[s], 128), F32)], axis=0
            )


def far_updates(ids, where, table, high, low, w, caps, starts, boxes, interpret=False):
    count, dof, slots, skel = w.shape
    red = dof - skel
    whole = lambda shape: pl.BlockSpec(shape, lambda b, *_: (0,) * len(shape))
    by_box = lambda shape: pl.BlockSpec((1,) + shape, lambda b, *_: (b,) + (0,) * len(shape))
    outs = [(64 * cap + 8, 128) for cap in caps]
    return pl.pallas_call(
        functools.partial(far_kernel, caps=caps, starts=starts, boxes=boxes),
        out_shape=[jax.ShapeDtypeStruct(shape, F32) for shape in outs],
        grid_spec=pltpu.PrefetchScalarGridSpec(
            num_scalar_prefetch=2,
            grid=(count,),
            in_specs=[row_spec(table)]
            + [by_box((red, dof)), by_box((red, dof)), by_box((dof, slots, skel))],
            out_specs=[whole(shape) for shape in outs],
            scratch_shapes=[
                pltpu.VMEM((starts[-1], 64, 128), F32),
                pltpu.VMEM((-(-starts[-1] // 8) * 8, 128), F32),
            ],
        ),
        compiler_params=pltpu.CompilerParams(vmem_limit_bytes=28 << 20),
        cost_estimate=pl.CostEstimate(flops=6 << 30, bytes_accessed=8 << 20, transcendentals=0),
        interpret=interpret,
        name="far_updates",
    )(ids, where, table, high, low, w)


def near_kernel(ids_ref, where_ref, high_ref, low_ref, last_high_ref, last_low_ref, w_ref, *rest):
    updated_ref, sib_outs, sib = rest[0], rest[1:-1], rest[-1]
    box = pl.program_id(0)
    this_sib = where_ref[1]

    @pl.when(box == 0)
    def _():
        sib[...] = jnp.zeros_like(sib)

    slots = w_ref.shape[2]
    by_slot = jnp.swapaxes(w_ref[0], 0, 1)
    coupled_slots = []
    for first in range(0, slots, 2):
        pair = jnp.concatenate([by_slot[first], by_slot[first + 1]], axis=1)
        coupled = dot_bf16(last_high_ref[0], pair) + dot_bf16(last_low_ref[0], pair)
        coupled_slots += [coupled[:, :128].astype(BF16), coupled[:, 128:].astype(BF16)]
        if first >= NSIB:
            continue
        for s, update in enumerate(slot_updates(high_ref, low_ref, pair)):
            other = ids_ref[box, first + s]
            child = other & 1
            body, tail = pack_symmetric(update, child.astype(F32))
            place = ((((other >> 1) & 3) - this_sib) & 3) * 2 + child
            rows = pl.ds(pl.multiple_of(box * 128, 128), 128)
            sib[place, rows, :] = coupled[:, 128 * s : 128 * s + 128]
            sib[place, 256:320, :] = sib[place, 256:320, :] + body
            sib[place, 320:321, :] = sib[place, 320:321, :] + tail
    updated_ref[0] = jnp.swapaxes(jnp.stack(coupled_slots), 0, 1)

    @pl.when(box == pl.num_programs(0) - 1)
    def _():
        for i, out in enumerate(sib_outs):
            out[...] = sib[2 * i : 2 * i + 2]


def near_updates(ids, where, high, low, w, interpret=False):
    count, dof, slots, skel = w.shape
    red = dof - skel
    by_box = lambda shape: pl.BlockSpec((1,) + shape, lambda b, *_: (b,) + (0,) * len(shape))
    last = pl.BlockSpec((1, skel, dof), lambda b, *_: (b, red // skel, 0))
    return pl.pallas_call(
        near_kernel,
        out_shape=(
            [jax.ShapeDtypeStruct((count, skel, slots, skel), BF16)]
            + [jax.ShapeDtypeStruct((2, 328, 128), F32)] * 4
        ),
        grid_spec=pltpu.PrefetchScalarGridSpec(
            num_scalar_prefetch=2,
            grid=(count,),
            in_specs=[
                by_box((red, dof)),
                by_box((red, dof)),
                last,
                last,
                by_box((dof, slots, skel)),
            ],
            out_specs=[by_box((skel, slots, skel))]
            + [pl.BlockSpec((2, 328, 128), lambda b, *_: (0, 0, 0))] * 4,
            scratch_shapes=[pltpu.VMEM((8, 328, 128), F32)],
        ),
        compiler_params=pltpu.CompilerParams(vmem_limit_bytes=28 << 20),
        cost_estimate=pl.CostEstimate(flops=3 << 30, bytes_accessed=8 << 20, transcendentals=0),
        interpret=interpret,
        name="near_updates",
    )(ids, where, high, low, high, low, w)


def route_kernel(where_ref, table_ref, *rest, caps, starts, boxes):
    got, outs, sums = rest[: len(caps)], rest[len(caps) : -1], rest[-1]
    row = where_ref[0] & 7
    sums[...] = jnp.zeros_like(sums)
    for s, block in enumerate(got):
        for j in range(caps[s]):
            shift = table_ref[row, boxes + starts[s] + j]
            body = block[64 * j : 64 * j + 64]
            tail = block[64 * caps[s] + j : 64 * caps[s] + j + 1]
            second = tail[:, 64:65]
            share = jnp.broadcast_to(second, body.shape)
            row_share = jnp.broadcast_to(second, tail.shape)
            sums[shift, 0:64] = sums[shift, 0:64] + body * (1.0 - share)
            sums[shift, 64:128] = sums[shift, 64:128] + body * share
            sums[shift, 128:129] = sums[shift, 128:129] + tail * (1.0 - row_share)
            sums[shift, 129:130] = sums[shift, 129:130] + tail * row_share
    for out, shifts in zip(outs, ROUTES):
        for i, shift in enumerate(shifts):
            out[PAIR * i : PAIR * (i + 1)] = sums[shift]


PAIR = 136
ROUTES = ((0,), (1, 3), (7, 5), (4,), (2,), (6,))


def route(where, table, got, caps, starts, boxes, interpret=False):
    whole = lambda shape: pl.BlockSpec(shape, lambda b, *_: (0,) * len(shape))
    outs = [(PAIR * len(shifts), 128) for shifts in ROUTES]
    return pl.pallas_call(
        functools.partial(route_kernel, caps=caps, starts=starts, boxes=boxes),
        out_shape=[jax.ShapeDtypeStruct(shape, F32) for shape in outs],
        grid_spec=pltpu.PrefetchScalarGridSpec(
            num_scalar_prefetch=1,
            grid=(1,),
            in_specs=[row_spec(table)] + [whole(block.shape) for block in got],
            out_specs=[whole(shape) for shape in outs],
            scratch_shapes=[pltpu.VMEM((Z, PAIR, 128), F32)],
        ),
        compiler_params=pltpu.CompilerParams(vmem_limit_bytes=16 << 20),
        cost_estimate=pl.CostEstimate(flops=1 << 22, bytes_accessed=2 << 20, transcendentals=0),
        interpret=interpret,
        name="route",
    )(where, table, *got)


def fold_kernel(up_ref, down_ref, two_ref, six_ref, out_two, out_six):
    out_two[...] = two_ref[...] + up_ref[PAIR:]
    out_six[...] = six_ref[...] + down_ref[PAIR:]


def fold(up, down, two, six, interpret=False):
    vmem = pl.BlockSpec(memory_space=pltpu.VMEM)
    return pl.pallas_call(
        fold_kernel,
        out_shape=[jax.ShapeDtypeStruct((PAIR, 128), F32)] * 2,
        in_specs=[vmem] * 4,
        out_specs=[vmem] * 2,
        compiler_params=pltpu.CompilerParams(vmem_limit_bytes=4 << 20),
        cost_estimate=pl.CostEstimate(flops=1 << 17, bytes_accessed=1 << 18, transcendentals=0),
        interpret=interpret,
        name="fold",
    )(up, down, two, six)


def assemble_kernel(where_ref, own_ref, *rest):
    far = rest[:-8]
    kept = rest[-8:-4]
    got = rest[-4:-1]
    out_ref = rest[-1]
    sibs = [kept[0]] + list(got)
    skeleton = []
    for c in range(2):
        body = sum(block[64 * c : 64 * c + 64] for block in far)
        tail = sum(block[128 + c : 129 + c] for block in far)
        for other in sibs:
            body = body + other[c, 256:320, :]
            tail = tail + other[c, 320:321, :]
        skeleton.append(own_ref[c] - unpack_symmetric(body, tail))
    here = where_ref[1]
    wide = lambda ref: jnp.concatenate([ref[0, 0:256, :], ref[1, 0:256, :]], axis=1)
    zero = jnp.zeros((128, 128), F32)
    first = wide(kept[0]) + jnp.concatenate(
        [
            jnp.concatenate([skeleton[0], zero], axis=1),
            jnp.concatenate([zero, skeleton[1]], axis=1),
        ],
        axis=0,
    )
    out_ref[:, pl.ds(pl.multiple_of(here * 256, 256), 256)] = 0.5 * (first + first.T)
    for s in range(1, 4):
        column = (here + 4 - s) & 3
        block = 0.5 * (wide(kept[4 - s]) + wide(got[s - 1]).T)
        out_ref[:, pl.ds(pl.multiple_of(column * 256, 256), 256)] = block


def assemble(where, own, far, kept, got, interpret=False):
    vmem = pl.BlockSpec(memory_space=pltpu.VMEM)
    args = [own, *far, *kept, *got]
    return pl.pallas_call(
        assemble_kernel,
        out_shape=jax.ShapeDtypeStruct((256, 1024), F32),
        in_specs=[pl.BlockSpec(memory_space=pltpu.SMEM)] + [vmem] * len(args),
        out_specs=vmem,
        compiler_params=pltpu.CompilerParams(vmem_limit_bytes=24 << 20),
        interpret=interpret,
        name="assemble",
    )(where, *args)


def on_device(self_blocks, orders, interpolation, couplings, neighbours):
    boxes = lax.axis_size("box")
    sibs = lax.axis_size("sib")
    parent, sib = lax.axis_index("box"), lax.axis_index("sib")
    count = orders.shape[1]
    slots = couplings.shape[3]
    where = jnp.stack([parent, sib]).astype(jnp.int32)
    plans, caps, starts = plan(boxes, (slots - NSIB) * count // 2)
    table = jnp.asarray(plans)
    high, low, own = factor(self_blocks[0], orders[0], interpolation[0])
    ids = neighbours[0]
    sent = far_updates(ids, where, table, high, low, couplings[0], caps, starts, boxes)

    def shifted(block, dy, dz, dc):
        moves = []
        for i in range(boxes):
            y, z, c = place_of(i)
            moves.append((i, box_of(y + dy, z + dz, c + dc)))
        return lax.ppermute(block, "box", moves)

    got = [sent[0]]
    for (dy, dc), block in zip(STAGES[1:], sent[1:]):
        got.append(shifted(block, dy, 0, dc))
    updated, *kept = near_updates(ids, where, high, low, couplings[0])
    sib_got = [
        lax.ppermute(kept[s], "sib", [(i, (i + s) % sibs) for i in range(sibs)])
        for s in range(1, sibs)
    ]
    here, up, down, four, two, six = route(where, table, got, caps, starts, boxes)
    up = shifted(up, 0, 1, 0)
    down = shifted(down, 0, -1, 0)
    four = shifted(four, 0, 4, 0)
    two, six = fold(up, down, two, six)
    far = [here, up, down, four, shifted(two, 0, 2, 0), shifted(six, 0, -2, 0)]
    rows = assemble(where, own, far, kept, sib_got)
    return updated[None], rows[None]


def solution(mesh):
    return jax.shard_map(
        on_device,
        mesh=mesh,
        in_specs=(
            P("box", "sib", None, None),
            P("box", "sib", None),
            P("box", "sib", None, None),
            P("box", "sib", None, None, None),
            P("box", "sib", None),
        ),
        out_specs=(P("box", "sib", None, None, None), P("box", "sib", None)),
        check_vma=False,
    )
```

```python
import functools
import jax
import jax.numpy as jnp
import numpy as np
from jax import lax
from jax.experimental import pallas as pl
from jax.experimental.pallas import tpu as pltpu
from jax.sharding import PartitionSpec as P


NSIB = 4
HIGH = lax.Precision.HIGHEST
F32 = jnp.float32
BF16 = jnp.bfloat16
NT = (((1,), (1,)), ((), ()))
NN = (((1,), (0,)), ((), ()))


def dot_high(a, b, dims=NN):
    return lax.dot_general(a, b, dims, precision=HIGH, preferred_element_type=F32)


def dot_bf16(a, b, dims=NN):
    return lax.dot_general(a, b, dims, preferred_element_type=F32)


def split2(x):
    hi = x.astype(BF16)
    return hi, (x - hi.astype(F32)).astype(BF16)


def split3(x):
    hi = x.astype(BF16)
    rest = x - hi.astype(F32)
    mid = rest.astype(BF16)
    return hi, mid, (rest - mid.astype(F32)).astype(BF16)


def iota(shape, dim):
    return lax.broadcasted_iota(jnp.int32, shape, dim)


def spread(x, lane):
    return jnp.take_along_axis(x, jnp.full(x.shape, lane, jnp.int32), axis=1)


def eliminate_rows(panels, nexts, base):
    shape = panels[0].shape
    lane, sub = iota(shape, 1), iota(shape, 0)
    panels, nexts = list(panels), list(nexts)
    columns = [[spread(panel, base + t) for t in range(8)] for panel in panels]
    next_columns = [[spread(rows, base + t) for t in range(8)] for rows in nexts]
    inverses = [jnp.ones(shape, F32) for _ in panels]
    for t in range(8):
        here = lane == base + t
        one = (sub == t).astype(F32)
        for b, panel in enumerate(panels):
            column = columns[b][t]
            inverse = 1.0 / jnp.broadcast_to(column[t : t + 1, :], shape)
            inverses[b] = jnp.where(sub == t, inverse, inverses[b])
            ratio = jnp.where(sub > t, column, 0.0) * inverse
            row = jnp.where(here, 1.0, jnp.broadcast_to(panel[t : t + 1, :], shape))
            if nexts:
                next_ratio = next_columns[b][t] * inverse
            for u in range(t + 1, 8):
                later = columns[b][u]
                pivot_row = jnp.broadcast_to(later[t : t + 1, :], shape)
                columns[b][u] = later - ratio * pivot_row
                if nexts:
                    next_columns[b][u] = next_columns[b][u] - next_ratio * pivot_row
            panels[b] = jnp.where(here, one, panel) - ratio * row
            if nexts:
                nexts[b] = jnp.where(here, 0.0, nexts[b]) - next_ratio * row
    return panels, nexts, inverses


def invert_cholesky(blocks):
    count, size, span = len(blocks), blocks[0].shape[0], 32
    shape = (8, size)
    lane, sub = iota(shape, 1), iota(shape, 0)
    rows = [[block[8 * g : 8 * g + 8, :] for g in range(size // 8)] for block in blocks]
    out = [[] for _ in blocks]
    for start in range(0, size, span):
        end = start + span
        finals, scaled_rows = [[] for _ in blocks], [[] for _ in blocks]
        for g in range(start // 8, end // 8):
            base = 8 * g
            nexts = [rows[b][g + 1] for b in range(count)] if base + 8 < end else []
            panels, nexts, inverses = eliminate_rows([r[g] for r in rows], nexts, base)
            for b in range(count):
                panel = panels[b]
                scaled = panel * inverses[b]
                beyond = lane > sub + base
                out[b].append(jnp.where(beyond, 0.0, panel * jnp.sqrt(inverses[b])))
                finals[b].append(panel)
                scaled_rows[b].append(jnp.where(beyond & (lane < end), 0.0, scaled))
                if not nexts:
                    continue
                rows[b][g + 1] = nexts[b]
                scaled = jnp.where(beyond & (lane < base + 8), 0.0, scaled)
                clear = (lane >= base) & (lane < base + 8)
                for i in range(g + 2, end // 8):
                    terms = [
                        jnp.take_along_axis(
                            jnp.broadcast_to(panel[t : t + 1, :], shape), 8 * i + sub, axis=1
                        )
                        * jnp.broadcast_to(scaled[t : t + 1, :], shape)
                        for t in range(8)
                    ]
                    while len(terms) > 1:
                        terms = [terms[j] + terms[j + 1] for j in range(0, len(terms), 2)]
                    rows[b][i] = jnp.where(clear, 0.0, rows[b][i]) - terms[0]
        if end < size:
            clear = (lane >= start) & (lane < end)
            for b in range(count):
                factors = jnp.concatenate(finals[b], axis=0).T[end:]
                update = dot_high(factors, jnp.concatenate(scaled_rows[b], axis=0))
                for i in range(end // 8, size // 8):
                    k = 8 * i - end
                    rows[b][i] = jnp.where(clear, 0.0, rows[b][i]) - update[k : k + 8]
    return [jnp.concatenate(parts, axis=0) for parts in out]


def pick_lanes(x, order):
    rows, width = x.shape
    chunks = [x[:, 128 * q : 128 * (q + 1)] for q in range(width // 128)]
    parts = []
    for q in range(width // 128):
        wanted = jnp.broadcast_to(order[:, 128 * q : 128 * (q + 1)], (rows, 128))
        lane, chunk = wanted & 127, wanted >> 7
        picked = jnp.take_along_axis(chunks[0], lane, axis=1)
        for c in range(1, len(chunks)):
            picked = jnp.where(chunk == c, jnp.take_along_axis(chunks[c], lane, axis=1), picked)
        parts.append(picked)
    return jnp.concatenate(parts, axis=1)


def one_hot_rows(order, rows, width):
    column = jnp.broadcast_to(order.astype(F32), (128, order.shape[1])).T
    lanes = iota((rows, 128), 1).astype(F32)
    return jnp.concatenate(
        [(column[:rows] == lanes + 128.0 * q).astype(F32) for q in range(width // 128)], axis=1
    )


def factor_kernel(
    blocks_hbm,
    orders_hbm,
    interp_hbm,
    high_ref,
    low_ref,
    own_ref,
    blocks_ref,
    orders_ref,
    interp_ref,
    work,
    aug,
    sems,
):
    count, dof, _ = blocks_ref.shape
    skel, red = interp_ref.shape[1:]
    order_copy = pltpu.make_async_copy(orders_hbm, orders_ref, sems.at[0])
    block_copy = lambda b: pltpu.make_async_copy(
        blocks_hbm.at[b], blocks_ref.at[b], sems.at[1 + b]
    )
    interp_copy = lambda b: pltpu.make_async_copy(
        interp_hbm.at[b], interp_ref.at[b], sems.at[1 + count + b]
    )
    order_copy.start()
    for b in range(count):
        block_copy(b).start()
        interp_copy(b).start()
    order_copy.wait()

    @pl.loop(0, count)
    def _(b):
        order = orders_ref[pl.ds(b, 1), :]
        block_copy(b).wait()
        ordered = pick_lanes(pick_lanes(blocks_ref[b], order).T, order)
        interp_copy(b).wait()
        a_ss = ordered[:skel, :skel]
        a_sr = ordered[:skel, skel:]
        interp = interp_ref[b]
        interp_t = interp.T
        bar_sr = a_sr - dot_high(a_ss, interp)
        left = jnp.concatenate([a_sr.T, interp_t], axis=1)
        right = jnp.concatenate([interp, bar_sr], axis=0)
        work[b] = ordered[skel:, skel:] - dot_high(left, right)
        place = one_hot_rows(order, dof, dof)
        place_s = place[:skel].astype(BF16)
        pieces = [dot_bf16(part, place_s) for part in split3(interp_t)]
        aug[b, :, :dof] = place[skel:] - (pieces[0] + (pieces[1] + pieces[2]))
        aug[b, :, dof:] = bar_sr.T
        own_ref[b] = a_ss

    panels = red // 128
    for k in range(panels):
        lo, hi = 128 * k, 128 * (k + 1)
        inverses = invert_cholesky([work[b, lo:hi, lo:hi] for b in range(count)])
        for b in range(count):
            solved = dot_high(inverses[b], aug[b, lo:hi, :])
            aug[b, lo:hi, :] = solved
            if hi < red:
                panel = dot_high(work[b, hi:, lo:hi], inverses[b], NT)
                work[b, hi:, hi:] = work[b, hi:, hi:] - dot_high(panel, panel, NT)
                aug[b, hi:, :] = aug[b, hi:, :] - dot_high(panel, solved)
    for b in range(count):
        solved_t = aug[b, :, dof:].T
        own_ref[b] = own_ref[b] - dot_high(solved_t, aug[b, :, dof:])
        grid_high, grid_low = split2(aug[b, :, :dof])
        high_ref[b, :red] = grid_high
        low_ref[b, :red] = grid_low
        place_s = one_hot_rows(orders_ref[b : b + 1, :], skel, dof)
        last_high, last_low = split2(place_s - dot_high(solved_t, aug[b, :, :dof]))
        high_ref[b, red:] = last_high
        low_ref[b, red:] = last_low


def factor(self_blocks, orders, interpolation, interpret=False):
    count, dof, _ = self_blocks.shape
    skel, red = interpolation.shape[1:]
    return pl.pallas_call(
        factor_kernel,
        out_shape=(
            jax.ShapeDtypeStruct((count, dof, dof), BF16),
            jax.ShapeDtypeStruct((count, dof, dof), BF16),
            jax.ShapeDtypeStruct((count, skel, skel), F32),
        ),
        in_specs=[pl.BlockSpec(memory_space=pltpu.HBM)] * 3,
        scratch_shapes=[
            pltpu.VMEM((count, dof, dof), F32),
            pltpu.VMEM((count, dof), jnp.int32),
            pltpu.VMEM((count, skel, red), F32),
            pltpu.VMEM((count, red, red), F32),
            pltpu.VMEM((count, red, dof + skel), F32),
            pltpu.SemaphoreType.DMA((2 * count + 1,)),
        ],
        compiler_params=pltpu.CompilerParams(vmem_limit_bytes=51 << 20),
        cost_estimate=pl.CostEstimate(flops=8 << 30, bytes_accessed=6 << 20, transcendentals=0),
        interpret=interpret,
        name="factor",
    )(self_blocks, orders, interpolation)


def pack_symmetric(block, flag):
    half = block.shape[0] // 2
    top, bottom = block[:half], block[half:]
    lane, row = iota((half, 128), 1), iota((half, 128), 0)
    turned = pltpu.roll(bottom, half, 1)
    body = jnp.where((lane >= half) | (lane > row), top, turned)
    diagonal = jnp.sum(jnp.where(lane == row, top, 0.0), axis=0, keepdims=True)
    return body, jnp.where(iota((1, 128), 1) < half, diagonal, flag)


def unpack_symmetric(body, tail):
    half = 64
    lane, row = iota((half, 128), 1), iota((half, 128), 0)
    upper = jnp.where((lane >= half) | (lane > row), body, 0.0)
    inner = jnp.where(lane < half, body, 0.0)
    lower = pltpu.roll(jnp.where(lane < row, inner, 0.0), half, 1)
    strict = jnp.concatenate([upper, lower], axis=0)
    first = jnp.where(lane == row, jnp.broadcast_to(tail, (half, 128)), 0.0)
    second = pltpu.roll(jnp.where(lane == row, inner, 0.0), half, 1)
    return strict + strict.T + jnp.concatenate([first, second], axis=0)


Y, Z, C = 4, 8, 2
STAGES = [(dy, dc) for dy in range(Y) for dc in range(C)]
TABLE = 128


def place_of(box):
    return box // (Z * C), box // C % Z, box % C


def box_of(y, z, c):
    return (y % Y * Z + z % Z) * C + c % C


def plan(boxes, reach):
    steps = [(j * (boxes // 2)) // reach for j in range(1, reach + 1)]
    steps += [boxes - (j * ((boxes - 1) // 2)) // reach for j in range(1, reach + 1)]
    lists = []
    for box in range(boxes):
        y, z, c = place_of(box)
        by_stage = {stage: [] for stage in STAGES}
        for step in steps:
            ty, tz, tc = place_of((box + step) % boxes)
            by_stage[(ty - y) % Y, (tc - c) % C].append((step, (tz - z) % Z))
        lists.append(by_stage)
    caps = [max(len(found[stage]) for found in lists) for stage in STAGES]
    starts = np.concatenate([[0], np.cumsum(caps)]).tolist()
    table = np.zeros((boxes, TABLE), np.int32)
    for box in range(boxes):
        y, z, c = place_of(box)
        for s, stage in enumerate(STAGES):
            for j, (step, _) in enumerate(lists[box][stage]):
                table[box, step] = starts[s] + j
            source = lists[box_of(y - stage[0], z, c - stage[1])]
            for j, (_, shift) in enumerate(source[stage]):
                table[box, boxes + starts[s] + j] = shift
    return table, caps, starts


def row_spec(table):
    return pl.BlockSpec(
        (8, table.shape[1]), lambda *args: (args[-1][0] // 8, 0), memory_space=pltpu.SMEM
    )


def gram(z_t):
    high, low = split2(z_t)
    return dot_bf16(high, high, NT) + (dot_bf16(high, low, NT) + dot_bf16(low, high, NT))


def slot_updates(high_ref, low_ref, slot_pair):
    product = dot_bf16(high_ref[0], slot_pair) + dot_bf16(low_ref[0], slot_pair)
    both = gram(product.T)
    return both[:128, :128], both[128:, 128:]


def far_kernel(ids_ref, where_ref, table_ref, high_ref, low_ref, w_ref, *rest, caps, starts, boxes):
    outs, (bodies, tails) = rest[: len(caps)], rest[len(caps) :]
    box = pl.program_id(0)
    parent = where_ref[0]

    @pl.when(box == 0)
    def _():
        bodies[...] = jnp.zeros_like(bodies)
        tails[...] = jnp.zeros_like(tails)

    slots = w_ref.shape[2]
    by_slot = jnp.swapaxes(w_ref[0], 0, 1)
    for first in range(NSIB, slots, 2):
        pair = jnp.concatenate([by_slot[first], by_slot[first + 1]], axis=1)
        for s, update in enumerate(slot_updates(high_ref, low_ref, pair)):
            other = ids_ref[box, first + s]
            body, tail = pack_symmetric(update, (other & 1).astype(F32))
            place = table_ref[parent & 7, ((other >> 3) - parent) & (boxes - 1)]
            bodies[place] = body
            tails[pl.ds(place, 1), :] = tail

    @pl.when(box == pl.num_programs(0) - 1)
    def _():
        for s, out in enumerate(outs):
            for j in range(caps[s]):
                out[64 * j : 64 * j + 64] = bodies[starts[s] + j]
            out[64 * caps[s] : 64 * caps[s] + 8] = jnp.concatenate(
                [tails[starts[s] : starts[s] + caps[s]], jnp.zeros((8 - caps[s], 128), F32)], axis=0
            )


def far_updates(ids, where, table, high, low, w, caps, starts, boxes, interpret=False):
    count, dof, slots, skel = w.shape
    red = dof - skel
    whole = lambda shape: pl.BlockSpec(shape, lambda b, *_: (0,) * len(shape))
    by_box = lambda shape: pl.BlockSpec((1,) + shape, lambda b, *_: (b,) + (0,) * len(shape))
    outs = [(64 * cap + 8, 128) for cap in caps]
    return pl.pallas_call(
        functools.partial(far_kernel, caps=caps, starts=starts, boxes=boxes),
        out_shape=[jax.ShapeDtypeStruct(shape, F32) for shape in outs],
        grid_spec=pltpu.PrefetchScalarGridSpec(
            num_scalar_prefetch=2,
            grid=(count,),
            in_specs=[row_spec(table)]
            + [by_box((red, dof)), by_box((red, dof)), by_box((dof, slots, skel))],
            out_specs=[whole(shape) for shape in outs],
            scratch_shapes=[
                pltpu.VMEM((starts[-1], 64, 128), F32),
                pltpu.VMEM((-(-starts[-1] // 8) * 8, 128), F32),
            ],
        ),
        compiler_params=pltpu.CompilerParams(vmem_limit_bytes=28 << 20),
        cost_estimate=pl.CostEstimate(flops=6 << 30, bytes_accessed=8 << 20, transcendentals=0),
        interpret=interpret,
        name="far_updates",
    )(ids, where, table, high, low, w)


def near_kernel(ids_ref, where_ref, high_ref, low_ref, w_ref, *rest):
    near_ref, sib_outs, sib = rest[0], rest[1:-1], rest[-1]
    box = pl.program_id(0)
    this_sib = where_ref[1]
    red = high_ref.shape[1] - w_ref.shape[3]

    @pl.when(box == 0)
    def _():
        sib[...] = jnp.zeros_like(sib)

    by_slot = jnp.swapaxes(w_ref[0, :, :8], 0, 1)
    for first in range(0, NSIB, 2):
        pair = jnp.concatenate([by_slot[first], by_slot[first + 1]], axis=1)
        product = dot_bf16(high_ref[0], pair) + dot_bf16(low_ref[0], pair)
        both = gram(product[:red].T)
        for s in range(2):
            part = slice(128 * s, 128 * (s + 1))
            coupled = product[red:, part]
            near_ref[0, first + s] = coupled
            other = ids_ref[box, first + s]
            child = other & 1
            body, tail = pack_symmetric(both[part, part], child.astype(F32))
            place = ((((other >> 1) & 3) - this_sib) & 3) * 2 + child
            rows = pl.ds(pl.multiple_of(box * 128, 128), 128)
            sib[place, rows, :] = coupled
            sib[place, 256:320, :] = sib[place, 256:320, :] + body
            sib[place, 320:321, :] = sib[place, 320:321, :] + tail

    @pl.when(box == pl.num_programs(0) - 1)
    def _():
        for i, out in enumerate(sib_outs):
            out[...] = sib[2 * i : 2 * i + 2]


def near_updates(ids, where, high, low, w, interpret=False):
    count, dof, slots, skel = w.shape
    by_box = lambda shape: pl.BlockSpec((1,) + shape, lambda b, *_: (b,) + (0,) * len(shape))
    return pl.pallas_call(
        near_kernel,
        out_shape=(
            [jax.ShapeDtypeStruct((count, NSIB, skel, skel), F32)]
            + [jax.ShapeDtypeStruct((2, 328, 128), F32)] * 4
        ),
        grid_spec=pltpu.PrefetchScalarGridSpec(
            num_scalar_prefetch=2,
            grid=(count,),
            in_specs=[by_box((dof, dof)), by_box((dof, dof)), by_box((dof, slots, skel))],
            out_specs=[by_box((NSIB, skel, skel))]
            + [pl.BlockSpec((2, 328, 128), lambda b, *_: (0, 0, 0))] * 4,
            scratch_shapes=[pltpu.VMEM((8, 328, 128), F32)],
        ),
        compiler_params=pltpu.CompilerParams(vmem_limit_bytes=28 << 20),
        cost_estimate=pl.CostEstimate(flops=3 << 30, bytes_accessed=8 << 20, transcendentals=0),
        interpret=interpret,
        name="near_updates",
    )(ids, where, high, low, w)


def couple_kernel(high_ref, low_ref, near_ref, w_ref, updated_ref):
    slots = w_ref.shape[2]
    by_slot = jnp.swapaxes(w_ref[0], 0, 1)
    parts = [near_ref[0, k].astype(BF16) for k in range(NSIB)]
    for first in range(NSIB, slots, 2):
        pair = jnp.concatenate([by_slot[first], by_slot[first + 1]], axis=1)
        coupled = dot_bf16(high_ref[0], pair) + dot_bf16(low_ref[0], pair)
        parts += [coupled[:, :128].astype(BF16), coupled[:, 128:].astype(BF16)]
    updated_ref[0] = jnp.swapaxes(jnp.stack(parts), 0, 1)


def couple(high, low, near, w, interpret=False):
    count, dof, slots, skel = w.shape
    by_box = lambda shape: pl.BlockSpec((1,) + shape, lambda b: (b,) + (0,) * len(shape))
    last = pl.BlockSpec((1, skel, dof), lambda b: (b, dof // skel - 1, 0))
    return pl.pallas_call(
        couple_kernel,
        out_shape=jax.ShapeDtypeStruct((count, skel, slots, skel), BF16),
        grid=(count,),
        in_specs=[last, last, by_box((NSIB, skel, skel)), by_box((dof, slots, skel))],
        out_specs=by_box((skel, slots, skel)),
        compiler_params=pltpu.CompilerParams(vmem_limit_bytes=28 << 20),
        cost_estimate=pl.CostEstimate(flops=2 << 30, bytes_accessed=6 << 20, transcendentals=0),
        interpret=interpret,
        name="couple",
    )(high, low, near, w)


def route_kernel(where_ref, table_ref, *rest, caps, starts, boxes):
    got, outs, sums = rest[: len(caps)], rest[len(caps) : -1], rest[-1]
    row = where_ref[0] & 7
    sums[...] = jnp.zeros_like(sums)
    for s, block in enumerate(got):
        for j in range(caps[s]):
            shift = table_ref[row, boxes + starts[s] + j]
            body = block[64 * j : 64 * j + 64]
            tail = block[64 * caps[s] + j : 64 * caps[s] + j + 1]
            second = tail[:, 64:65]
            share = jnp.broadcast_to(second, body.shape)
            row_share = jnp.broadcast_to(second, tail.shape)
            sums[shift, 0:64] = sums[shift, 0:64] + body * (1.0 - share)
            sums[shift, 64:128] = sums[shift, 64:128] + body * share
            sums[shift, 128:129] = sums[shift, 128:129] + tail * (1.0 - row_share)
            sums[shift, 129:130] = sums[shift, 129:130] + tail * row_share
    for out, shifts in zip(outs, ROUTES):
        for i, shift in enumerate(shifts):
            out[PAIR * i : PAIR * (i + 1)] = sums[shift]


PAIR = 136
ROUTES = ((0,), (1, 3), (7, 5), (4,), (2,), (6,))


def route(where, table, got, caps, starts, boxes, interpret=False):
    whole = lambda shape: pl.BlockSpec(shape, lambda b, *_: (0,) * len(shape))
    outs = [(PAIR * len(shifts), 128) for shifts in ROUTES]
    return pl.pallas_call(
        functools.partial(route_kernel, caps=caps, starts=starts, boxes=boxes),
        out_shape=[jax.ShapeDtypeStruct(shape, F32) for shape in outs],
        grid_spec=pltpu.PrefetchScalarGridSpec(
            num_scalar_prefetch=1,
            grid=(1,),
            in_specs=[row_spec(table)] + [whole(block.shape) for block in got],
            out_specs=[whole(shape) for shape in outs],
            scratch_shapes=[pltpu.VMEM((Z, PAIR, 128), F32)],
        ),
        compiler_params=pltpu.CompilerParams(vmem_limit_bytes=16 << 20),
        cost_estimate=pl.CostEstimate(flops=1 << 22, bytes_accessed=2 << 20, transcendentals=0),
        interpret=interpret,
        name="route",
    )(where, table, *got)


def fold_kernel(up_ref, down_ref, two_ref, six_ref, out_two, out_six):
    out_two[...] = two_ref[...] + up_ref[PAIR:]
    out_six[...] = six_ref[...] + down_ref[PAIR:]


def fold(up, down, two, six, interpret=False):
    vmem = pl.BlockSpec(memory_space=pltpu.VMEM)
    return pl.pallas_call(
        fold_kernel,
        out_shape=[jax.ShapeDtypeStruct((PAIR, 128), F32)] * 2,
        in_specs=[vmem] * 4,
        out_specs=[vmem] * 2,
        compiler_params=pltpu.CompilerParams(vmem_limit_bytes=4 << 20),
        cost_estimate=pl.CostEstimate(flops=1 << 17, bytes_accessed=1 << 18, transcendentals=0),
        interpret=interpret,
        name="fold",
    )(up, down, two, six)


def assemble_kernel(where_ref, own_ref, *rest):
    far = rest[:-8]
    kept = rest[-8:-4]
    got = rest[-4:-1]
    out_ref = rest[-1]
    sibs = [kept[0]] + list(got)
    skeleton = []
    for c in range(2):
        body = sum(block[64 * c : 64 * c + 64] for block in far)
        tail = sum(block[128 + c : 129 + c] for block in far)
        for other in sibs:
            body = body + other[c, 256:320, :]
            tail = tail + other[c, 320:321, :]
        skeleton.append(own_ref[c] - unpack_symmetric(body, tail))
    here = where_ref[1]
    wide = lambda ref: jnp.concatenate([ref[0, 0:256, :], ref[1, 0:256, :]], axis=1)
    zero = jnp.zeros((128, 128), F32)
    first = wide(kept[0]) + jnp.concatenate(
        [
            jnp.concatenate([skeleton[0], zero], axis=1),
            jnp.concatenate([zero, skeleton[1]], axis=1),
        ],
        axis=0,
    )
    out_ref[:, pl.ds(pl.multiple_of(here * 256, 256), 256)] = 0.5 * (first + first.T)
    for s in range(1, 4):
        column = (here + 4 - s) & 3
        block = 0.5 * (wide(kept[4 - s]) + wide(got[s - 1]).T)
        out_ref[:, pl.ds(pl.multiple_of(column * 256, 256), 256)] = block


def assemble(where, own, far, kept, got, interpret=False):
    vmem = pl.BlockSpec(memory_space=pltpu.VMEM)
    args = [own, *far, *kept, *got]
    return pl.pallas_call(
        assemble_kernel,
        out_shape=jax.ShapeDtypeStruct((256, 1024), F32),
        in_specs=[pl.BlockSpec(memory_space=pltpu.SMEM)] + [vmem] * len(args),
        out_specs=vmem,
        compiler_params=pltpu.CompilerParams(vmem_limit_bytes=24 << 20),
        interpret=interpret,
        name="assemble",
    )(where, *args)


def on_device(self_blocks, orders, interpolation, couplings, neighbours):
    boxes = lax.axis_size("box")
    sibs = lax.axis_size("sib")
    parent, sib = lax.axis_index("box"), lax.axis_index("sib")
    count = orders.shape[1]
    slots = couplings.shape[3]
    where = jnp.stack([parent, sib]).astype(jnp.int32)
    plans, caps, starts = plan(boxes, (slots - NSIB) * count // 2)
    table = jnp.asarray(plans)
    high, low, own = factor(self_blocks[0], orders[0], interpolation[0])
    ids = neighbours[0]
    sent = far_updates(ids, where, table, high, low, couplings[0], caps, starts, boxes)

    def shifted(block, dy, dz, dc):
        moves = []
        for i in range(boxes):
            y, z, c = place_of(i)
            moves.append((i, box_of(y + dy, z + dz, c + dc)))
        return lax.ppermute(block, "box", moves)

    got = [sent[0]]
    for (dy, dc), block in zip(STAGES[1:], sent[1:]):
        got.append(shifted(block, dy, 0, dc))
    near, *kept = near_updates(ids, where, high, low, couplings[0])
    sib_got = []
    for s in range(1, sibs):
        moves = [(i, (i + s) % sibs) for i in range(sibs)]
        sib_got.append(lax.ppermute(kept[s], "sib", moves))
    here, up, down, four, two, six = route(where, table, got, caps, starts, boxes)
    up = shifted(up, 0, 1, 0)
    down = shifted(down, 0, -1, 0)
    four = shifted(four, 0, 4, 0)
    two, six = fold(up, down, two, six)
    two = shifted(two, 0, 2, 0)
    six = shifted(six, 0, -2, 0)
    far = [here, up, down, four, two, six]
    updated = couple(high, low, near, couplings[0])
    rows = assemble(where, own, far, kept, sib_got)
    return updated[None], rows[None]


def solution(mesh):
    return jax.shard_map(
        on_device,
        mesh=mesh,
        in_specs=(
            P("box", "sib", None, None),
            P("box", "sib", None),
            P("box", "sib", None, None),
            P("box", "sib", None, None, None),
            P("box", "sib", None),
        ),
        out_specs=(P("box", "sib", None, None, None), P("box", "sib", None)),
        check_vma=False,
    )
```

```python
import functools
import jax
import jax.numpy as jnp
import numpy as np
from jax import lax
from jax.experimental import pallas as pl
from jax.experimental.pallas import tpu as pltpu
from jax.sharding import PartitionSpec as P


NSIB = 4
HIGH = lax.Precision.HIGHEST
F32 = jnp.float32
BF16 = jnp.bfloat16
NT = (((1,), (1,)), ((), ()))
NN = (((1,), (0,)), ((), ()))


def dot_high(a, b, dims=NN):
    return lax.dot_general(a, b, dims, precision=HIGH, preferred_element_type=F32)


def dot_bf16(a, b, dims=NN):
    return lax.dot_general(a, b, dims, preferred_element_type=F32)


def split2(x):
    hi = x.astype(BF16)
    return hi, (x - hi.astype(F32)).astype(BF16)


def split3(x):
    hi = x.astype(BF16)
    rest = x - hi.astype(F32)
    mid = rest.astype(BF16)
    return hi, mid, (rest - mid.astype(F32)).astype(BF16)


def dot3(a, b, dims=NN):
    ah, al = split2(a)
    bh, bl = split2(b)
    return dot_bf16(ah, bh, dims) + (dot_bf16(ah, bl, dims) + dot_bf16(al, bh, dims))


def iota(shape, dim):
    return lax.broadcasted_iota(jnp.int32, shape, dim)


def spread(x, lane):
    return jnp.take_along_axis(x, jnp.full(x.shape, lane, jnp.int32), axis=1)


def eliminate_rows(panels, nexts, base):
    shape = panels[0].shape
    lane, sub = iota(shape, 1), iota(shape, 0)
    panels, nexts = list(panels), list(nexts)
    columns = [[spread(panel, base + t) for t in range(8)] for panel in panels]
    next_columns = [[spread(rows, base + t) for t in range(8)] for rows in nexts]
    inverses = [jnp.ones(shape, F32) for _ in panels]
    for t in range(8):
        here = lane == base + t
        one = (sub == t).astype(F32)
        for b, panel in enumerate(panels):
            column = columns[b][t]
            inverse = 1.0 / jnp.broadcast_to(column[t : t + 1, :], shape)
            inverses[b] = jnp.where(sub == t, inverse, inverses[b])
            ratio = jnp.where(sub > t, column, 0.0) * inverse
            row = jnp.where(here, 1.0, jnp.broadcast_to(panel[t : t + 1, :], shape))
            if nexts:
                next_ratio = next_columns[b][t] * inverse
            for u in range(t + 1, 8):
                later = columns[b][u]
                pivot_row = jnp.broadcast_to(later[t : t + 1, :], shape)
                columns[b][u] = later - ratio * pivot_row
                if nexts:
                    next_columns[b][u] = next_columns[b][u] - next_ratio * pivot_row
            panels[b] = jnp.where(here, one, panel) - ratio * row
            if nexts:
                nexts[b] = jnp.where(here, 0.0, nexts[b]) - next_ratio * row
    return panels, nexts, inverses


def invert_cholesky(blocks):
    count, size, span = len(blocks), blocks[0].shape[0], 32
    shape = (8, size)
    lane, sub = iota(shape, 1), iota(shape, 0)
    rows = [[block[8 * g : 8 * g + 8, :] for g in range(size // 8)] for block in blocks]
    out = [[] for _ in blocks]
    for start in range(0, size, span):
        end = start + span
        finals, scaled_rows = [[] for _ in blocks], [[] for _ in blocks]
        for g in range(start // 8, end // 8):
            base = 8 * g
            nexts = [rows[b][g + 1] for b in range(count)] if base + 8 < end else []
            panels, nexts, inverses = eliminate_rows([r[g] for r in rows], nexts, base)
            for b in range(count):
                panel = panels[b]
                scaled = panel * inverses[b]
                beyond = lane > sub + base
                out[b].append(jnp.where(beyond, 0.0, panel * jnp.sqrt(inverses[b])))
                finals[b].append(panel)
                scaled_rows[b].append(jnp.where(beyond & (lane < end), 0.0, scaled))
                if not nexts:
                    continue
                rows[b][g + 1] = nexts[b]
                scaled = jnp.where(beyond & (lane < base + 8), 0.0, scaled)
                clear = (lane >= base) & (lane < base + 8)
                for i in range(g + 2, end // 8):
                    terms = [
                        jnp.take_along_axis(
                            jnp.broadcast_to(panel[t : t + 1, :], shape), 8 * i + sub, axis=1
                        )
                        * jnp.broadcast_to(scaled[t : t + 1, :], shape)
                        for t in range(8)
                    ]
                    while len(terms) > 1:
                        terms = [terms[j] + terms[j + 1] for j in range(0, len(terms), 2)]
                    rows[b][i] = jnp.where(clear, 0.0, rows[b][i]) - terms[0]
        if end < size:
            clear = (lane >= start) & (lane < end)
            for b in range(count):
                factors = jnp.concatenate(finals[b], axis=0).T[end:]
                update = dot_high(factors, jnp.concatenate(scaled_rows[b], axis=0))
                for i in range(end // 8, size // 8):
                    k = 8 * i - end
                    rows[b][i] = jnp.where(clear, 0.0, rows[b][i]) - update[k : k + 8]
    return [jnp.concatenate(parts, axis=0) for parts in out]


def pick_lanes(x, order):
    rows, width = x.shape
    chunks = [x[:, 128 * q : 128 * (q + 1)] for q in range(width // 128)]
    parts = []
    for q in range(width // 128):
        wanted = jnp.broadcast_to(order[:, 128 * q : 128 * (q + 1)], (rows, 128))
        lane, chunk = wanted & 127, wanted >> 7
        picked = jnp.take_along_axis(chunks[0], lane, axis=1)
        for c in range(1, len(chunks)):
            picked = jnp.where(chunk == c, jnp.take_along_axis(chunks[c], lane, axis=1), picked)
        parts.append(picked)
    return jnp.concatenate(parts, axis=1)


def one_hot_rows(order, rows, width):
    column = jnp.broadcast_to(order.astype(F32), (128, order.shape[1])).T
    lanes = iota((rows, 128), 1).astype(F32)
    return jnp.concatenate(
        [(column[:rows] == lanes + 128.0 * q).astype(F32) for q in range(width // 128)], axis=1
    )


def factor_kernel(
    blocks_hbm,
    orders_hbm,
    interp_hbm,
    high_ref,
    low_ref,
    own_ref,
    blocks_ref,
    orders_ref,
    interp_ref,
    work,
    aug,
    sems,
):
    count, dof, _ = blocks_ref.shape
    skel, red = interp_ref.shape[1:]
    order_copy = pltpu.make_async_copy(orders_hbm, orders_ref, sems.at[0])
    block_copy = lambda b: pltpu.make_async_copy(
        blocks_hbm.at[b], blocks_ref.at[b], sems.at[1 + b]
    )
    interp_copy = lambda b: pltpu.make_async_copy(
        interp_hbm.at[b], interp_ref.at[b], sems.at[1 + count + b]
    )
    order_copy.start()
    for b in range(count):
        block_copy(b).start()
        interp_copy(b).start()
    order_copy.wait()

    @pl.loop(0, count)
    def _(b):
        order = orders_ref[pl.ds(b, 1), :]
        block_copy(b).wait()
        ordered = pick_lanes(pick_lanes(blocks_ref[b], order).T, order)
        interp_copy(b).wait()
        a_ss = ordered[:skel, :skel]
        a_sr = ordered[:skel, skel:]
        interp = interp_ref[b]
        interp_t = interp.T
        bar_sr = a_sr - dot_high(a_ss, interp)
        left = jnp.concatenate([a_sr.T, interp_t], axis=1)
        right = jnp.concatenate([interp, bar_sr], axis=0)
        work[b] = ordered[skel:, skel:] - dot_high(left, right)
        place = one_hot_rows(order, dof, dof)
        place_s = place[:skel].astype(BF16)
        pieces = [dot_bf16(part, place_s) for part in split3(interp_t)]
        aug[b, :, :dof] = place[skel:] - (pieces[0] + (pieces[1] + pieces[2]))
        aug[b, :, dof:] = bar_sr.T
        own_ref[b] = a_ss

    panels = red // 128
    for k in range(panels):
        lo, hi = 128 * k, 128 * (k + 1)
        inverses = invert_cholesky([work[b, lo:hi, lo:hi] for b in range(count)])
        for b in range(count):
            solved = dot_high(inverses[b], aug[b, lo:hi, :])
            aug[b, lo:hi, :] = solved
            if hi < red:
                panel = dot_high(work[b, hi:, lo:hi], inverses[b], NT)
                work[b, hi:, hi:] = work[b, hi:, hi:] - dot_high(panel, panel, NT)
                aug[b, hi:, :] = aug[b, hi:, :] - dot_high(panel, solved)
    for b in range(count):
        solved_t = aug[b, :, dof:].T
        own_ref[b] = own_ref[b] - dot_high(solved_t, aug[b, :, dof:])
        grid_high, grid_low = split2(aug[b, :, :dof])
        high_ref[b, :red] = grid_high
        low_ref[b, :red] = grid_low
        place_s = one_hot_rows(orders_ref[b : b + 1, :], skel, dof)
        last_high, last_low = split2(place_s - dot3(solved_t, aug[b, :, :dof]))
        high_ref[b, red:] = last_high
        low_ref[b, red:] = last_low


def factor(self_blocks, orders, interpolation, interpret=False):
    count, dof, _ = self_blocks.shape
    skel, red = interpolation.shape[1:]
    return pl.pallas_call(
        factor_kernel,
        out_shape=(
            jax.ShapeDtypeStruct((count, dof, dof), BF16),
            jax.ShapeDtypeStruct((count, dof, dof), BF16),
            jax.ShapeDtypeStruct((count, skel, skel), F32),
        ),
        in_specs=[pl.BlockSpec(memory_space=pltpu.HBM)] * 3,
        scratch_shapes=[
            pltpu.VMEM((count, dof, dof), F32),
            pltpu.VMEM((count, dof), jnp.int32),
            pltpu.VMEM((count, skel, red), F32),
            pltpu.VMEM((count, red, red), F32),
            pltpu.VMEM((count, red, dof + skel), F32),
            pltpu.SemaphoreType.DMA((2 * count + 1,)),
        ],
        compiler_params=pltpu.CompilerParams(vmem_limit_bytes=51 << 20),
        cost_estimate=pl.CostEstimate(flops=8 << 30, bytes_accessed=6 << 20, transcendentals=0),
        interpret=interpret,
        name="factor",
    )(self_blocks, orders, interpolation)


def pack_symmetric(block, flag):
    half = block.shape[0] // 2
    top, bottom = block[:half], block[half:]
    lane, row = iota((half, 128), 1), iota((half, 128), 0)
    turned = pltpu.roll(bottom, half, 1)
    body = jnp.where((lane >= half) | (lane > row), top, turned)
    diagonal = jnp.sum(jnp.where(lane == row, top, 0.0), axis=0, keepdims=True)
    return body, jnp.where(iota((1, 128), 1) < half, diagonal, flag)


def unpack_symmetric(body, tail):
    half = 64
    lane, row = iota((half, 128), 1), iota((half, 128), 0)
    upper = jnp.where((lane >= half) | (lane > row), body, 0.0)
    inner = jnp.where(lane < half, body, 0.0)
    lower = pltpu.roll(jnp.where(lane < row, inner, 0.0), half, 1)
    strict = jnp.concatenate([upper, lower], axis=0)
    first = jnp.where(lane == row, jnp.broadcast_to(tail, (half, 128)), 0.0)
    second = pltpu.roll(jnp.where(lane == row, inner, 0.0), half, 1)
    return strict + strict.T + jnp.concatenate([first, second], axis=0)


Y, Z, C = 4, 8, 2
STAGES = [(dy, dc) for dy in range(Y) for dc in range(C)]
TABLE = 128


def place_of(box):
    return box // (Z * C), box // C % Z, box % C


def box_of(y, z, c):
    return (y % Y * Z + z % Z) * C + c % C


def plan(boxes, reach):
    steps = [(j * (boxes // 2)) // reach for j in range(1, reach + 1)]
    steps += [boxes - (j * ((boxes - 1) // 2)) // reach for j in range(1, reach + 1)]
    lists = []
    for box in range(boxes):
        y, z, c = place_of(box)
        by_stage = {stage: [] for stage in STAGES}
        for step in steps:
            ty, tz, tc = place_of((box + step) % boxes)
            by_stage[(ty - y) % Y, (tc - c) % C].append((step, (tz - z) % Z))
        lists.append(by_stage)
    caps = [max(len(found[stage]) for found in lists) for stage in STAGES]
    starts = np.concatenate([[0], np.cumsum(caps)]).tolist()
    table = np.zeros((boxes, TABLE), np.int32)
    for box in range(boxes):
        y, z, c = place_of(box)
        for s, stage in enumerate(STAGES):
            for j, (step, _) in enumerate(lists[box][stage]):
                table[box, step] = starts[s] + j
            source = lists[box_of(y - stage[0], z, c - stage[1])]
            for j, (_, shift) in enumerate(source[stage]):
                table[box, boxes + starts[s] + j] = shift
    return table, caps, starts


def row_spec(table):
    return pl.BlockSpec(
        (8, table.shape[1]), lambda *args: (args[-1][0] // 8, 0), memory_space=pltpu.SMEM
    )


def gram(z_t):
    high, low = split2(z_t)
    return dot_bf16(high, high, NT) + (dot_bf16(high, low, NT) + dot_bf16(low, high, NT))


def slot_updates(high_ref, low_ref, slot_pair):
    product = dot_bf16(high_ref[0], slot_pair) + dot_bf16(low_ref[0], slot_pair)
    both = gram(product.T)
    return both[:128, :128], both[128:, 128:]


def far_kernel(ids_ref, where_ref, table_ref, high_ref, low_ref, w_ref, *rest, caps, starts, boxes):
    outs, (bodies, tails) = rest[: len(caps)], rest[len(caps) :]
    box = pl.program_id(0)
    parent = where_ref[0]

    @pl.when(box == 0)
    def _():
        bodies[...] = jnp.zeros_like(bodies)
        tails[...] = jnp.zeros_like(tails)

    slots = w_ref.shape[2]
    by_slot = jnp.swapaxes(w_ref[0], 0, 1)
    for first in range(NSIB, slots, 2):
        pair = jnp.concatenate([by_slot[first], by_slot[first + 1]], axis=1)
        for s, update in enumerate(slot_updates(high_ref, low_ref, pair)):
            other = ids_ref[box, first + s]
            body, tail = pack_symmetric(update, (other & 1).astype(F32))
            place = table_ref[parent & 7, ((other >> 3) - parent) & (boxes - 1)]
            bodies[place] = body
            tails[pl.ds(place, 1), :] = tail

    @pl.when(box == pl.num_programs(0) - 1)
    def _():
        for s, out in enumerate(outs):
            for j in range(caps[s]):
                out[64 * j : 64 * j + 64] = bodies[starts[s] + j]
            out[64 * caps[s] : 64 * caps[s] + 8] = jnp.concatenate(
                [tails[starts[s] : starts[s] + caps[s]], jnp.zeros((8 - caps[s], 128), F32)], axis=0
            )


def far_updates(ids, where, table, high, low, w, caps, starts, boxes, interpret=False):
    count, dof, slots, skel = w.shape
    red = dof - skel
    whole = lambda shape: pl.BlockSpec(shape, lambda b, *_: (0,) * len(shape))
    by_box = lambda shape: pl.BlockSpec((1,) + shape, lambda b, *_: (b,) + (0,) * len(shape))
    outs = [(64 * cap + 8, 128) for cap in caps]
    return pl.pallas_call(
        functools.partial(far_kernel, caps=caps, starts=starts, boxes=boxes),
        out_shape=[jax.ShapeDtypeStruct(shape, F32) for shape in outs],
        grid_spec=pltpu.PrefetchScalarGridSpec(
            num_scalar_prefetch=2,
            grid=(count,),
            in_specs=[row_spec(table)]
            + [by_box((red, dof)), by_box((red, dof)), by_box((dof, slots, skel))],
            out_specs=[whole(shape) for shape in outs],
            scratch_shapes=[
                pltpu.VMEM((starts[-1], 64, 128), F32),
                pltpu.VMEM((-(-starts[-1] // 8) * 8, 128), F32),
            ],
        ),
        compiler_params=pltpu.CompilerParams(vmem_limit_bytes=28 << 20),
        cost_estimate=pl.CostEstimate(flops=6 << 30, bytes_accessed=8 << 20, transcendentals=0),
        interpret=interpret,
        name="far_updates",
    )(ids, where, table, high, low, w)


def near_kernel(ids_ref, where_ref, high_ref, low_ref, w_ref, near_ref, *sib_outs):
    this_sib = where_ref[1]
    red = high_ref.shape[1] - w_ref.shape[3]
    count = w_ref.shape[0]
    sib = sib_outs[-1]
    sib[...] = jnp.zeros_like(sib)

    found = []
    for box in range(count):
        by_slot = jnp.swapaxes(w_ref[box, :, :8], 0, 1)
        for first in range(0, NSIB, 2):
            pair = jnp.concatenate([by_slot[first], by_slot[first + 1]], axis=1)
            product = dot_bf16(high_ref[box], pair) + dot_bf16(low_ref[box], pair)
            found.append((box, first, product[red:], gram(product[:red].T)))
    for box, first, last, both in found:
        for s in range(2):
            part = slice(128 * s, 128 * (s + 1))
            coupled = last[:, part]
            near_ref[box, first + s] = coupled
            other = ids_ref[box, first + s]
            child = other & 1
            body, tail = pack_symmetric(both[part, part], child.astype(F32))
            place = ((((other >> 1) & 3) - this_sib) & 3) * 2 + child
            rows = slice(128 * box, 128 * (box + 1))
            sib[place, rows, :] = coupled
            sib[place, 256:320, :] = sib[place, 256:320, :] + body
            sib[place, 320:321, :] = sib[place, 320:321, :] + tail

    for i, out in enumerate(sib_outs[:-1]):
        out[...] = sib[2 * i : 2 * i + 2]


def near_updates(ids, where, high, low, w, interpret=False):
    count, _, _, skel = w.shape
    return pl.pallas_call(
        near_kernel,
        out_shape=(
            [jax.ShapeDtypeStruct((count, NSIB, skel, skel), F32)]
            + [jax.ShapeDtypeStruct((2, 328, 128), F32)] * 4
        ),
        in_specs=[pl.BlockSpec(memory_space=pltpu.SMEM)] * 2
        + [pl.BlockSpec(memory_space=pltpu.VMEM)] * 3,
        out_specs=[pl.BlockSpec(memory_space=pltpu.VMEM)] * 5,
        scratch_shapes=[pltpu.VMEM((8, 328, 128), F32)],
        compiler_params=pltpu.CompilerParams(vmem_limit_bytes=28 << 20),
        cost_estimate=pl.CostEstimate(flops=3 << 30, bytes_accessed=8 << 20, transcendentals=0),
        interpret=interpret,
        name="near_updates",
    )(ids, where, high, low, w)


def couple_kernel(high_ref, low_ref, near_ref, w_ref, updated_ref):
    slots = w_ref.shape[2]
    by_slot = jnp.swapaxes(w_ref[0], 0, 1)
    parts = [near_ref[0, k].astype(BF16) for k in range(NSIB)]
    for first in range(NSIB, slots, 2):
        pair = jnp.concatenate([by_slot[first], by_slot[first + 1]], axis=1)
        coupled = dot_bf16(high_ref[0], pair) + dot_bf16(low_ref[0], pair)
        parts += [coupled[:, :128].astype(BF16), coupled[:, 128:].astype(BF16)]
    updated_ref[0] = jnp.swapaxes(jnp.stack(parts), 0, 1)


def couple(high, low, near, w, interpret=False):
    count, dof, slots, skel = w.shape
    by_box = lambda shape: pl.BlockSpec((1,) + shape, lambda b: (b,) + (0,) * len(shape))
    last = pl.BlockSpec((1, skel, dof), lambda b: (b, dof // skel - 1, 0))
    return pl.pallas_call(
        couple_kernel,
        out_shape=jax.ShapeDtypeStruct((count, skel, slots, skel), BF16),
        grid=(count,),
        in_specs=[last, last, by_box((NSIB, skel, skel)), by_box((dof, slots, skel))],
        out_specs=by_box((skel, slots, skel)),
        compiler_params=pltpu.CompilerParams(vmem_limit_bytes=28 << 20),
        cost_estimate=pl.CostEstimate(flops=2 << 30, bytes_accessed=6 << 20, transcendentals=0),
        interpret=interpret,
        name="couple",
    )(high, low, near, w)


def route_kernel(where_ref, table_ref, *rest, caps, starts, boxes):
    got, outs, sums = rest[: len(caps)], rest[len(caps) : -1], rest[-1]
    row = where_ref[0] & 7
    sums[...] = jnp.zeros_like(sums)
    for s, block in enumerate(got):
        for j in range(caps[s]):
            shift = table_ref[row, boxes + starts[s] + j]
            body = block[64 * j : 64 * j + 64]
            tail = block[64 * caps[s] + j : 64 * caps[s] + j + 1]
            second = tail[:, 64:65]
            share = jnp.broadcast_to(second, body.shape)
            row_share = jnp.broadcast_to(second, tail.shape)
            sums[shift, 0:64] = sums[shift, 0:64] + body * (1.0 - share)
            sums[shift, 64:128] = sums[shift, 64:128] + body * share
            sums[shift, 128:129] = sums[shift, 128:129] + tail * (1.0 - row_share)
            sums[shift, 129:130] = sums[shift, 129:130] + tail * row_share
    for out, shifts in zip(outs, ROUTES):
        for i, shift in enumerate(shifts):
            out[PAIR * i : PAIR * (i + 1)] = sums[shift]


PAIR = 136
ROUTES = ((0,), (1, 3), (7, 5), (4,), (2,), (6,))


def route(where, table, got, caps, starts, boxes, interpret=False):
    whole = lambda shape: pl.BlockSpec(shape, lambda b, *_: (0,) * len(shape))
    outs = [(PAIR * len(shifts), 128) for shifts in ROUTES]
    return pl.pallas_call(
        functools.partial(route_kernel, caps=caps, starts=starts, boxes=boxes),
        out_shape=[jax.ShapeDtypeStruct(shape, F32) for shape in outs],
        grid_spec=pltpu.PrefetchScalarGridSpec(
            num_scalar_prefetch=1,
            grid=(1,),
            in_specs=[row_spec(table)] + [whole(block.shape) for block in got],
            out_specs=[whole(shape) for shape in outs],
            scratch_shapes=[pltpu.VMEM((Z, PAIR, 128), F32)],
        ),
        compiler_params=pltpu.CompilerParams(vmem_limit_bytes=16 << 20),
        cost_estimate=pl.CostEstimate(flops=1 << 22, bytes_accessed=2 << 20, transcendentals=0),
        interpret=interpret,
        name="route",
    )(where, table, *got)


def fold_kernel(up_ref, down_ref, two_ref, six_ref, out_two, out_six):
    out_two[...] = two_ref[...] + up_ref[PAIR:]
    out_six[...] = six_ref[...] + down_ref[PAIR:]


def fold(up, down, two, six, interpret=False):
    vmem = pl.BlockSpec(memory_space=pltpu.VMEM)
    return pl.pallas_call(
        fold_kernel,
        out_shape=[jax.ShapeDtypeStruct((PAIR, 128), F32)] * 2,
        in_specs=[vmem] * 4,
        out_specs=[vmem] * 2,
        compiler_params=pltpu.CompilerParams(vmem_limit_bytes=4 << 20),
        cost_estimate=pl.CostEstimate(flops=1 << 17, bytes_accessed=1 << 18, transcendentals=0),
        interpret=interpret,
        name="fold",
    )(up, down, two, six)


def assemble_kernel(where_ref, own_ref, *rest):
    far = rest[:-8]
    kept = rest[-8:-4]
    got = rest[-4:-1]
    out_ref = rest[-1]
    sibs = [kept[0]] + list(got)
    skeleton = []
    for c in range(2):
        body = sum(block[64 * c : 64 * c + 64] for block in far)
        tail = sum(block[128 + c : 129 + c] for block in far)
        for other in sibs:
            body = body + other[c, 256:320, :]
            tail = tail + other[c, 320:321, :]
        skeleton.append(own_ref[c] - unpack_symmetric(body, tail))
    here = where_ref[1]
    wide = lambda ref: jnp.concatenate([ref[0, 0:256, :], ref[1, 0:256, :]], axis=1)
    zero = jnp.zeros((128, 128), F32)
    first = wide(kept[0]) + jnp.concatenate(
        [
            jnp.concatenate([skeleton[0], zero], axis=1),
            jnp.concatenate([zero, skeleton[1]], axis=1),
        ],
        axis=0,
    )
    out_ref[:, pl.ds(pl.multiple_of(here * 256, 256), 256)] = 0.5 * (first + first.T)
    for s in range(1, 4):
        column = (here + 4 - s) & 3
        block = 0.5 * (wide(kept[4 - s]) + wide(got[s - 1]).T)
        out_ref[:, pl.ds(pl.multiple_of(column * 256, 256), 256)] = block


def assemble(where, own, far, kept, got, interpret=False):
    vmem = pl.BlockSpec(memory_space=pltpu.VMEM)
    args = [own, *far, *kept, *got]
    return pl.pallas_call(
        assemble_kernel,
        out_shape=jax.ShapeDtypeStruct((256, 1024), F32),
        in_specs=[pl.BlockSpec(memory_space=pltpu.SMEM)] + [vmem] * len(args),
        out_specs=vmem,
        compiler_params=pltpu.CompilerParams(vmem_limit_bytes=24 << 20),
        interpret=interpret,
        name="assemble",
    )(where, *args)


def on_device(self_blocks, orders, interpolation, couplings, neighbours):
    boxes = lax.axis_size("box")
    sibs = lax.axis_size("sib")
    parent, sib = lax.axis_index("box"), lax.axis_index("sib")
    count = orders.shape[1]
    slots = couplings.shape[3]
    where = jnp.stack([parent, sib]).astype(jnp.int32)
    plans, caps, starts = plan(boxes, (slots - NSIB) * count // 2)
    table = jnp.asarray(plans)
    high, low, own = factor(self_blocks[0], orders[0], interpolation[0])
    ids = neighbours[0]
    sent = far_updates(ids, where, table, high, low, couplings[0], caps, starts, boxes)

    def shifted(block, dy, dz, dc):
        moves = []
        for i in range(boxes):
            y, z, c = place_of(i)
            moves.append((i, box_of(y + dy, z + dz, c + dc)))
        return lax.ppermute(block, "box", moves)

    got = [sent[0]]
    for (dy, dc), block in zip(STAGES[1:], sent[1:]):
        got.append(shifted(block, dy, 0, dc))
    near, *kept = near_updates(ids, where, high, low, couplings[0])
    sib_got = []
    for s in range(1, sibs):
        moves = [(i, (i + s) % sibs) for i in range(sibs)]
        sib_got.append(lax.ppermute(kept[s], "sib", moves))
    here, up, down, four, two, six = route(where, table, got, caps, starts, boxes)
    up = shifted(up, 0, 1, 0)
    down = shifted(down, 0, -1, 0)
    four = shifted(four, 0, 4, 0)
    two, six = fold(up, down, two, six)
    two = shifted(two, 0, 2, 0)
    six = shifted(six, 0, -2, 0)
    far = [here, up, down, four, two, six]
    updated = couple(high, low, near, couplings[0])
    rows = assemble(where, own, far, kept, sib_got)
    return updated[None], rows[None]


def solution(mesh):
    return jax.shard_map(
        on_device,
        mesh=mesh,
        in_specs=(
            P("box", "sib", None, None),
            P("box", "sib", None),
            P("box", "sib", None, None),
            P("box", "sib", None, None, None),
            P("box", "sib", None),
        ),
        out_specs=(P("box", "sib", None, None, None), P("box", "sib", None)),
        check_vma=False,
    )
```

```python
import functools
import jax
import jax.numpy as jnp
import numpy as np
from jax import lax
from jax.experimental import pallas as pl
from jax.experimental.pallas import tpu as pltpu
from jax.sharding import PartitionSpec as P


NSIB = 4
HIGH = lax.Precision.HIGHEST
F32 = jnp.float32
BF16 = jnp.bfloat16
NT = (((1,), (1,)), ((), ()))
NN = (((1,), (0,)), ((), ()))


def dot_high(a, b, dims=NN):
    return lax.dot_general(a, b, dims, precision=HIGH, preferred_element_type=F32)


def dot_bf16(a, b, dims=NN):
    return lax.dot_general(a, b, dims, preferred_element_type=F32)


def split2(x):
    hi = x.astype(BF16)
    return hi, (x - hi.astype(F32)).astype(BF16)


def split3(x):
    hi = x.astype(BF16)
    rest = x - hi.astype(F32)
    mid = rest.astype(BF16)
    return hi, mid, (rest - mid.astype(F32)).astype(BF16)


def dot3(a, b, dims=NN):
    ah, al = split2(a)
    bh, bl = split2(b)
    return dot_bf16(ah, bh, dims) + (dot_bf16(ah, bl, dims) + dot_bf16(al, bh, dims))


def iota(shape, dim):
    return lax.broadcasted_iota(jnp.int32, shape, dim)


def spread(x, lane):
    return jnp.take_along_axis(x, jnp.full(x.shape, lane, jnp.int32), axis=1)


def eliminate_rows(panels, nexts, base):
    shape = panels[0].shape
    lane, sub = iota(shape, 1), iota(shape, 0)
    panels, nexts = list(panels), list(nexts)
    columns = [[spread(panel, base + t) for t in range(8)] for panel in panels]
    next_columns = [[spread(rows, base + t) for t in range(8)] for rows in nexts]
    inverses = [jnp.ones(shape, F32) for _ in panels]
    for t in range(8):
        here = lane == base + t
        one = (sub == t).astype(F32)
        for b, panel in enumerate(panels):
            column = columns[b][t]
            inverse = 1.0 / jnp.broadcast_to(column[t : t + 1, :], shape)
            inverses[b] = jnp.where(sub == t, inverse, inverses[b])
            ratio = jnp.where(sub > t, column, 0.0) * inverse
            row = jnp.where(here, 1.0, jnp.broadcast_to(panel[t : t + 1, :], shape))
            if nexts:
                next_ratio = next_columns[b][t] * inverse
            for u in range(t + 1, 8):
                later = columns[b][u]
                pivot_row = jnp.broadcast_to(later[t : t + 1, :], shape)
                columns[b][u] = later - ratio * pivot_row
                if nexts:
                    next_columns[b][u] = next_columns[b][u] - next_ratio * pivot_row
            panels[b] = jnp.where(here, one, panel) - ratio * row
            if nexts:
                nexts[b] = jnp.where(here, 0.0, nexts[b]) - next_ratio * row
    return panels, nexts, inverses


def invert_cholesky(blocks):
    count, size, span = len(blocks), blocks[0].shape[0], 32
    shape = (8, size)
    lane, sub = iota(shape, 1), iota(shape, 0)
    rows = [[block[8 * g : 8 * g + 8, :] for g in range(size // 8)] for block in blocks]
    out = [[] for _ in blocks]
    for start in range(0, size, span):
        end = start + span
        finals, scaled_rows = [[] for _ in blocks], [[] for _ in blocks]
        for g in range(start // 8, end // 8):
            base = 8 * g
            nexts = [rows[b][g + 1] for b in range(count)] if base + 8 < end else []
            panels, nexts, inverses = eliminate_rows([r[g] for r in rows], nexts, base)
            for b in range(count):
                panel = panels[b]
                scaled = panel * inverses[b]
                beyond = lane > sub + base
                out[b].append(jnp.where(beyond, 0.0, panel * jnp.sqrt(inverses[b])))
                finals[b].append(panel)
                scaled_rows[b].append(jnp.where(beyond & (lane < end), 0.0, scaled))
                if not nexts:
                    continue
                rows[b][g + 1] = nexts[b]
                scaled = jnp.where(beyond & (lane < base + 8), 0.0, scaled)
                clear = (lane >= base) & (lane < base + 8)
                for i in range(g + 2, end // 8):
                    terms = [
                        jnp.take_along_axis(
                            jnp.broadcast_to(panel[t : t + 1, :], shape), 8 * i + sub, axis=1
                        )
                        * jnp.broadcast_to(scaled[t : t + 1, :], shape)
                        for t in range(8)
                    ]
                    while len(terms) > 1:
                        terms = [terms[j] + terms[j + 1] for j in range(0, len(terms), 2)]
                    rows[b][i] = jnp.where(clear, 0.0, rows[b][i]) - terms[0]
        if end < size:
            clear = (lane >= start) & (lane < end)
            for b in range(count):
                factors = jnp.concatenate(finals[b], axis=0).T[end:]
                update = dot_high(factors, jnp.concatenate(scaled_rows[b], axis=0))
                for i in range(end // 8, size // 8):
                    k = 8 * i - end
                    rows[b][i] = jnp.where(clear, 0.0, rows[b][i]) - update[k : k + 8]
    return [jnp.concatenate(parts, axis=0) for parts in out]


def pick_lanes(x, order):
    rows, width = x.shape
    chunks = [x[:, 128 * q : 128 * (q + 1)] for q in range(width // 128)]
    parts = []
    for q in range(width // 128):
        wanted = jnp.broadcast_to(order[:, 128 * q : 128 * (q + 1)], (rows, 128))
        lane, chunk = wanted & 127, wanted >> 7
        picked = jnp.take_along_axis(chunks[0], lane, axis=1)
        for c in range(1, len(chunks)):
            picked = jnp.where(chunk == c, jnp.take_along_axis(chunks[c], lane, axis=1), picked)
        parts.append(picked)
    return jnp.concatenate(parts, axis=1)


def one_hot_rows(order, rows, width):
    column = jnp.broadcast_to(order.astype(F32), (128, order.shape[1])).T
    lanes = iota((rows, 128), 1).astype(F32)
    return jnp.concatenate(
        [(column[:rows] == lanes + 128.0 * q).astype(F32) for q in range(width // 128)], axis=1
    )


def factor_kernel(
    blocks_hbm,
    orders_hbm,
    interp_hbm,
    high_ref,
    low_ref,
    own_ref,
    blocks_ref,
    orders_ref,
    interp_ref,
    work,
    aug,
    sems,
):
    count, dof, _ = blocks_ref.shape
    skel, red = interp_ref.shape[1:]
    order_copy = pltpu.make_async_copy(orders_hbm, orders_ref, sems.at[0])
    block_copy = lambda b: pltpu.make_async_copy(
        blocks_hbm.at[b], blocks_ref.at[b], sems.at[1 + b]
    )
    interp_copy = lambda b: pltpu.make_async_copy(
        interp_hbm.at[b], interp_ref.at[b], sems.at[1 + count + b]
    )
    order_copy.start()
    for b in range(count):
        block_copy(b).start()
        interp_copy(b).start()
    order_copy.wait()

    @pl.loop(0, count)
    def _(b):
        order = orders_ref[pl.ds(b, 1), :]
        block_copy(b).wait()
        ordered = pick_lanes(pick_lanes(blocks_ref[b], order).T, order)
        interp_copy(b).wait()
        a_ss = ordered[:skel, :skel]
        a_sr = ordered[:skel, skel:]
        interp = interp_ref[b]
        interp_t = interp.T
        bar_sr = a_sr - dot_high(a_ss, interp)
        left = jnp.concatenate([a_sr.T, interp_t], axis=1)
        right = jnp.concatenate([interp, bar_sr], axis=0)
        work[b] = ordered[skel:, skel:] - dot_high(left, right)
        place = one_hot_rows(order, dof, dof)
        place_s = place[:skel].astype(BF16)
        pieces = [dot_bf16(part, place_s) for part in split3(interp_t)]
        aug[b, :, :dof] = place[skel:] - (pieces[0] + (pieces[1] + pieces[2]))
        aug[b, :, dof:] = bar_sr.T
        own_ref[b] = a_ss

    panels = red // 128
    for k in range(panels):
        lo, hi = 128 * k, 128 * (k + 1)
        inverses = invert_cholesky([work[b, lo:hi, lo:hi] for b in range(count)])
        for b in range(count):
            solved = dot3(inverses[b], aug[b, lo:hi, :])
            aug[b, lo:hi, :] = solved
            if hi < red:
                panel = dot_high(work[b, hi:, lo:hi], inverses[b], NT)
                work[b, hi:, hi:] = work[b, hi:, hi:] - dot_high(panel, panel, NT)
                aug[b, hi:, :] = aug[b, hi:, :] - dot3(panel, solved)
    for b in range(count):
        solved_t = aug[b, :, dof:].T
        own_ref[b] = own_ref[b] - dot_high(solved_t, aug[b, :, dof:])
        grid_high, grid_low = split2(aug[b, :, :dof])
        high_ref[b, :red] = grid_high
        low_ref[b, :red] = grid_low
        place_s = one_hot_rows(orders_ref[b : b + 1, :], skel, dof)
        last_high, last_low = split2(place_s - dot3(solved_t, aug[b, :, :dof]))
        high_ref[b, red:] = last_high
        low_ref[b, red:] = last_low


def factor(self_blocks, orders, interpolation, interpret=False):
    count, dof, _ = self_blocks.shape
    skel, red = interpolation.shape[1:]
    return pl.pallas_call(
        factor_kernel,
        out_shape=(
            jax.ShapeDtypeStruct((count, dof, dof), BF16),
            jax.ShapeDtypeStruct((count, dof, dof), BF16),
            jax.ShapeDtypeStruct((count, skel, skel), F32),
        ),
        in_specs=[pl.BlockSpec(memory_space=pltpu.HBM)] * 3,
        scratch_shapes=[
            pltpu.VMEM((count, dof, dof), F32),
            pltpu.VMEM((count, dof), jnp.int32),
            pltpu.VMEM((count, skel, red), F32),
            pltpu.VMEM((count, red, red), F32),
            pltpu.VMEM((count, red, dof + skel), F32),
            pltpu.SemaphoreType.DMA((2 * count + 1,)),
        ],
        compiler_params=pltpu.CompilerParams(vmem_limit_bytes=51 << 20),
        cost_estimate=pl.CostEstimate(flops=8 << 30, bytes_accessed=6 << 20, transcendentals=0),
        interpret=interpret,
        name="factor",
    )(*[
        pltpu.with_memory_space_constraint(x, pltpu.HBM)
        for x in (self_blocks, orders, interpolation)
    ])


def pack_symmetric(block, flag):
    half = block.shape[0] // 2
    top, bottom = block[:half], block[half:]
    lane, row = iota((half, 128), 1), iota((half, 128), 0)
    turned = pltpu.roll(bottom, half, 1)
    body = jnp.where((lane >= half) | (lane > row), top, turned)
    diagonal = jnp.sum(jnp.where(lane == row, top, 0.0), axis=0, keepdims=True)
    return body, jnp.where(iota((1, 128), 1) < half, diagonal, flag)


def unpack_symmetric(body, tail):
    half = 64
    lane, row = iota((half, 128), 1), iota((half, 128), 0)
    upper = jnp.where((lane >= half) | (lane > row), body, 0.0)
    inner = jnp.where(lane < half, body, 0.0)
    lower = pltpu.roll(jnp.where(lane < row, inner, 0.0), half, 1)
    strict = jnp.concatenate([upper, lower], axis=0)
    first = jnp.where(lane == row, jnp.broadcast_to(tail, (half, 128)), 0.0)
    second = pltpu.roll(jnp.where(lane == row, inner, 0.0), half, 1)
    return strict + strict.T + jnp.concatenate([first, second], axis=0)


Y, Z, C = 4, 8, 2
STAGES = [(dy, dc) for dy in range(Y) for dc in range(C)]
TABLE = 128


def place_of(box):
    return box // (Z * C), box // C % Z, box % C


def box_of(y, z, c):
    return (y % Y * Z + z % Z) * C + c % C


def plan(boxes, reach):
    steps = [(j * (boxes // 2)) // reach for j in range(1, reach + 1)]
    steps += [boxes - (j * ((boxes - 1) // 2)) // reach for j in range(1, reach + 1)]
    lists = []
    for box in range(boxes):
        y, z, c = place_of(box)
        by_stage = {stage: [] for stage in STAGES}
        for step in steps:
            ty, tz, tc = place_of((box + step) % boxes)
            by_stage[(ty - y) % Y, (tc - c) % C].append((step, (tz - z) % Z))
        lists.append(by_stage)
    caps = [max(len(found[stage]) for found in lists) for stage in STAGES]
    starts = np.concatenate([[0], np.cumsum(caps)]).tolist()
    table = np.zeros((boxes, TABLE), np.int32)
    for box in range(boxes):
        y, z, c = place_of(box)
        for s, stage in enumerate(STAGES):
            for j, (step, _) in enumerate(lists[box][stage]):
                table[box, step] = starts[s] + j
            source = lists[box_of(y - stage[0], z, c - stage[1])]
            for j, (_, shift) in enumerate(source[stage]):
                table[box, boxes + starts[s] + j] = shift
    return table, caps, starts


def row_spec(table):
    return pl.BlockSpec(
        (8, table.shape[1]), lambda *args: (args[-1][0] // 8, 0), memory_space=pltpu.SMEM
    )


def gram(z_t):
    high, low = split2(z_t)
    return dot_bf16(high, high, NT) + (dot_bf16(high, low, NT) + dot_bf16(low, high, NT))


def slot_updates(high_ref, low_ref, slot_pair):
    product = dot_bf16(high_ref[0], slot_pair) + dot_bf16(low_ref[0], slot_pair)
    both = gram(product.T)
    return both[:128, :128], both[128:, 128:]


def far_kernel(ids_ref, where_ref, table_ref, high_ref, low_ref, w_ref, *rest, caps, starts, boxes):
    outs, (bodies, tails) = rest[: len(caps)], rest[len(caps) :]
    box = pl.program_id(0)
    parent = where_ref[0]

    @pl.when(box == 0)
    def _():
        bodies[...] = jnp.zeros_like(bodies)
        tails[...] = jnp.zeros_like(tails)

    slots = w_ref.shape[2]
    by_slot = jnp.swapaxes(w_ref[0], 0, 1)
    for first in range(NSIB, slots, 2):
        pair = jnp.concatenate([by_slot[first], by_slot[first + 1]], axis=1)
        for s, update in enumerate(slot_updates(high_ref, low_ref, pair)):
            other = ids_ref[box, first + s]
            body, tail = pack_symmetric(update, (other & 1).astype(F32))
            place = table_ref[parent & 7, ((other >> 3) - parent) & (boxes - 1)]
            bodies[place] = body
            tails[pl.ds(place, 1), :] = tail

    @pl.when(box == pl.num_programs(0) - 1)
    def _():
        for s, out in enumerate(outs):
            for j in range(caps[s]):
                out[64 * j : 64 * j + 64] = bodies[starts[s] + j]
            out[64 * caps[s] : 64 * caps[s] + 8] = jnp.concatenate(
                [tails[starts[s] : starts[s] + caps[s]], jnp.zeros((8 - caps[s], 128), F32)], axis=0
            )


def far_updates(ids, where, table, high, low, w, caps, starts, boxes, interpret=False):
    count, dof, slots, skel = w.shape
    red = dof - skel
    whole = lambda shape: pl.BlockSpec(shape, lambda b, *_: (0,) * len(shape))
    by_box = lambda shape: pl.BlockSpec((1,) + shape, lambda b, *_: (b,) + (0,) * len(shape))
    outs = [(64 * cap + 8, 128) for cap in caps]
    return pl.pallas_call(
        functools.partial(far_kernel, caps=caps, starts=starts, boxes=boxes),
        out_shape=[jax.ShapeDtypeStruct(shape, F32) for shape in outs],
        grid_spec=pltpu.PrefetchScalarGridSpec(
            num_scalar_prefetch=2,
            grid=(count,),
            in_specs=[row_spec(table)]
            + [by_box((red, dof)), by_box((red, dof)), by_box((dof, slots, skel))],
            out_specs=[whole(shape) for shape in outs],
            scratch_shapes=[
                pltpu.VMEM((starts[-1], 64, 128), F32),
                pltpu.VMEM((-(-starts[-1] // 8) * 8, 128), F32),
            ],
        ),
        compiler_params=pltpu.CompilerParams(vmem_limit_bytes=28 << 20),
        cost_estimate=pl.CostEstimate(flops=6 << 30, bytes_accessed=8 << 20, transcendentals=0),
        interpret=interpret,
        name="far_updates",
    )(ids, where, table, high, low, w)


def near_kernel(ids_ref, where_ref, high_ref, low_ref, w_ref, near_ref, *sib_outs):
    this_sib = where_ref[1]
    red = high_ref.shape[1] - w_ref.shape[3]
    count = w_ref.shape[0]
    sib = sib_outs[-1]
    sib[...] = jnp.zeros_like(sib)

    found = []
    for box in range(count):
        by_slot = jnp.swapaxes(w_ref[box, :, :8], 0, 1)
        for first in range(0, NSIB, 2):
            pair = jnp.concatenate([by_slot[first], by_slot[first + 1]], axis=1)
            product = dot_bf16(high_ref[box], pair) + dot_bf16(low_ref[box], pair)
            found.append((box, first, product[red:], gram(product[:red].T)))
    for box, first, last, both in found:
        for s in range(2):
            part = slice(128 * s, 128 * (s + 1))
            coupled = last[:, part]
            near_ref[box, first + s] = coupled
            other = ids_ref[box, first + s]
            child = other & 1
            body, tail = pack_symmetric(both[part, part], child.astype(F32))
            place = ((((other >> 1) & 3) - this_sib) & 3) * 2 + child
            rows = slice(128 * box, 128 * (box + 1))
            sib[place, rows, :] = coupled
            sib[place, 256:320, :] = sib[place, 256:320, :] + body
            sib[place, 320:321, :] = sib[place, 320:321, :] + tail

    for i, out in enumerate(sib_outs[:-1]):
        out[...] = sib[2 * i : 2 * i + 2]


def near_updates(ids, where, high, low, w, interpret=False):
    count, _, _, skel = w.shape
    return pl.pallas_call(
        near_kernel,
        out_shape=(
            [jax.ShapeDtypeStruct((count, NSIB, skel, skel), F32)]
            + [jax.ShapeDtypeStruct((2, 328, 128), F32)] * 4
        ),
        in_specs=[pl.BlockSpec(memory_space=pltpu.SMEM)] * 2
        + [pl.BlockSpec(memory_space=pltpu.VMEM)] * 3,
        out_specs=[pl.BlockSpec(memory_space=pltpu.VMEM)] * 5,
        scratch_shapes=[pltpu.VMEM((8, 328, 128), F32)],
        compiler_params=pltpu.CompilerParams(vmem_limit_bytes=28 << 20),
        cost_estimate=pl.CostEstimate(flops=3 << 30, bytes_accessed=8 << 20, transcendentals=0),
        interpret=interpret,
        name="near_updates",
    )(ids, where, high, low, w)


def couple_kernel(high_ref, low_ref, near_ref, w_ref, updated_ref):
    slots = w_ref.shape[2]
    by_slot = jnp.swapaxes(w_ref[0], 0, 1)
    parts = [near_ref[0, k].astype(BF16) for k in range(NSIB)]
    for first in range(NSIB, slots, 2):
        pair = jnp.concatenate([by_slot[first], by_slot[first + 1]], axis=1)
        coupled = dot_bf16(high_ref[0], pair) + dot_bf16(low_ref[0], pair)
        parts += [coupled[:, :128].astype(BF16), coupled[:, 128:].astype(BF16)]
    updated_ref[0] = jnp.swapaxes(jnp.stack(parts), 0, 1)


def couple(high, low, near, w, interpret=False):
    count, dof, slots, skel = w.shape
    by_box = lambda shape: pl.BlockSpec((1,) + shape, lambda b: (b,) + (0,) * len(shape))
    last = pl.BlockSpec((1, skel, dof), lambda b: (b, dof // skel - 1, 0))
    return pl.pallas_call(
        couple_kernel,
        out_shape=jax.ShapeDtypeStruct((count, skel, slots, skel), BF16),
        grid=(count,),
        in_specs=[last, last, by_box((NSIB, skel, skel)), by_box((dof, slots, skel))],
        out_specs=by_box((skel, slots, skel)),
        compiler_params=pltpu.CompilerParams(vmem_limit_bytes=28 << 20),
        cost_estimate=pl.CostEstimate(flops=2 << 30, bytes_accessed=6 << 20, transcendentals=0),
        interpret=interpret,
        name="couple",
    )(high, low, near, w)


def route_kernel(where_ref, table_ref, *rest, caps, starts, boxes):
    got, outs, sums = rest[: len(caps)], rest[len(caps) : -1], rest[-1]
    row = where_ref[0] & 7
    sums[...] = jnp.zeros_like(sums)
    for s, block in enumerate(got):
        for j in range(caps[s]):
            shift = table_ref[row, boxes + starts[s] + j]
            body = block[64 * j : 64 * j + 64]
            tail = block[64 * caps[s] + j : 64 * caps[s] + j + 1]
            second = tail[:, 64:65]
            share = jnp.broadcast_to(second, body.shape)
            row_share = jnp.broadcast_to(second, tail.shape)
            sums[shift, 0:64] = sums[shift, 0:64] + body * (1.0 - share)
            sums[shift, 64:128] = sums[shift, 64:128] + body * share
            sums[shift, 128:129] = sums[shift, 128:129] + tail * (1.0 - row_share)
            sums[shift, 129:130] = sums[shift, 129:130] + tail * row_share
    for out, shifts in zip(outs, ROUTES):
        for i, shift in enumerate(shifts):
            out[PAIR * i : PAIR * (i + 1)] = sums[shift]


PAIR = 136
ROUTES = ((0,), (1, 3), (7, 5), (4,), (2,), (6,))


def route(where, table, got, caps, starts, boxes, interpret=False):
    whole = lambda shape: pl.BlockSpec(shape, lambda b, *_: (0,) * len(shape))
    outs = [(PAIR * len(shifts), 128) for shifts in ROUTES]
    return pl.pallas_call(
        functools.partial(route_kernel, caps=caps, starts=starts, boxes=boxes),
        out_shape=[jax.ShapeDtypeStruct(shape, F32) for shape in outs],
        grid_spec=pltpu.PrefetchScalarGridSpec(
            num_scalar_prefetch=1,
            grid=(1,),
            in_specs=[row_spec(table)] + [whole(block.shape) for block in got],
            out_specs=[whole(shape) for shape in outs],
            scratch_shapes=[pltpu.VMEM((Z, PAIR, 128), F32)],
        ),
        compiler_params=pltpu.CompilerParams(vmem_limit_bytes=16 << 20),
        cost_estimate=pl.CostEstimate(flops=1 << 22, bytes_accessed=2 << 20, transcendentals=0),
        interpret=interpret,
        name="route",
    )(where, table, *got)


def fold_kernel(up_ref, down_ref, two_ref, six_ref, out_two, out_six):
    out_two[...] = two_ref[...] + up_ref[PAIR:]
    out_six[...] = six_ref[...] + down_ref[PAIR:]


def fold(up, down, two, six, interpret=False):
    vmem = pl.BlockSpec(memory_space=pltpu.VMEM)
    return pl.pallas_call(
        fold_kernel,
        out_shape=[jax.ShapeDtypeStruct((PAIR, 128), F32)] * 2,
        in_specs=[vmem] * 4,
        out_specs=[vmem] * 2,
        compiler_params=pltpu.CompilerParams(vmem_limit_bytes=4 << 20),
        cost_estimate=pl.CostEstimate(flops=1 << 17, bytes_accessed=1 << 18, transcendentals=0),
        interpret=interpret,
        name="fold",
    )(up, down, two, six)


def assemble_kernel(where_ref, own_ref, *rest):
    far = rest[:-8]
    kept = rest[-8:-4]
    got = rest[-4:-1]
    out_ref = rest[-1]
    sibs = [kept[0]] + list(got)
    skeleton = []
    for c in range(2):
        body = sum(block[64 * c : 64 * c + 64] for block in far)
        tail = sum(block[128 + c : 129 + c] for block in far)
        for other in sibs:
            body = body + other[c, 256:320, :]
            tail = tail + other[c, 320:321, :]
        skeleton.append(own_ref[c] - unpack_symmetric(body, tail))
    here = where_ref[1]
    wide = lambda ref: jnp.concatenate([ref[0, 0:256, :], ref[1, 0:256, :]], axis=1)
    zero = jnp.zeros((128, 128), F32)
    first = wide(kept[0]) + jnp.concatenate(
        [
            jnp.concatenate([skeleton[0], zero], axis=1),
            jnp.concatenate([zero, skeleton[1]], axis=1),
        ],
        axis=0,
    )
    out_ref[:, pl.ds(pl.multiple_of(here * 256, 256), 256)] = 0.5 * (first + first.T)
    for s in range(1, 4):
        column = (here + 4 - s) & 3
        block = 0.5 * (wide(kept[4 - s]) + wide(got[s - 1]).T)
        out_ref[:, pl.ds(pl.multiple_of(column * 256, 256), 256)] = block


def assemble(where, own, far, kept, got, interpret=False):
    vmem = pl.BlockSpec(memory_space=pltpu.VMEM)
    args = [own, *far, *kept, *got]
    return pl.pallas_call(
        assemble_kernel,
        out_shape=jax.ShapeDtypeStruct((256, 1024), F32),
        in_specs=[pl.BlockSpec(memory_space=pltpu.SMEM)] + [vmem] * len(args),
        out_specs=vmem,
        compiler_params=pltpu.CompilerParams(vmem_limit_bytes=24 << 20),
        interpret=interpret,
        name="assemble",
    )(where, *args)


def on_device(self_blocks, orders, interpolation, couplings, neighbours):
    boxes = lax.axis_size("box")
    sibs = lax.axis_size("sib")
    parent, sib = lax.axis_index("box"), lax.axis_index("sib")
    count = orders.shape[1]
    slots = couplings.shape[3]
    where = jnp.stack([parent, sib]).astype(jnp.int32)
    plans, caps, starts = plan(boxes, (slots - NSIB) * count // 2)
    table = jnp.asarray(plans)
    high, low, own = factor(self_blocks[0], orders[0], interpolation[0])
    ids = neighbours[0]
    sent = far_updates(ids, where, table, high, low, couplings[0], caps, starts, boxes)

    def shifted(block, dy, dz, dc):
        moves = []
        for i in range(boxes):
            y, z, c = place_of(i)
            moves.append((i, box_of(y + dy, z + dz, c + dc)))
        return lax.ppermute(block, "box", moves)

    got = [sent[0]]
    for (dy, dc), block in zip(STAGES[1:], sent[1:]):
        got.append(shifted(block, dy, 0, dc))
    near, *kept = near_updates(ids, where, high, low, couplings[0])
    sib_got = []
    for s in range(1, sibs):
        moves = [(i, (i + s) % sibs) for i in range(sibs)]
        sib_got.append(lax.ppermute(kept[s], "sib", moves))
    here, up, down, four, two, six = route(where, table, got, caps, starts, boxes)
    up = shifted(up, 0, 1, 0)
    down = shifted(down, 0, -1, 0)
    four = shifted(four, 0, 4, 0)
    two, six = fold(up, down, two, six)
    two = shifted(two, 0, 2, 0)
    six = shifted(six, 0, -2, 0)
    far = [here, up, down, four, two, six]
    updated = couple(high, low, near, couplings[0])
    rows = assemble(where, own, far, kept, sib_got)
    return updated[None], rows[None]


def solution(mesh):
    return jax.shard_map(
        on_device,
        mesh=mesh,
        in_specs=(
            P("box", "sib", None, None),
            P("box", "sib", None),
            P("box", "sib", None, None),
            P("box", "sib", None, None, None),
            P("box", "sib", None),
        ),
        out_specs=(P("box", "sib", None, None, None), P("box", "sib", None)),
        check_vma=False,
    )
```

```python
import functools
import jax
import jax.numpy as jnp
import numpy as np
from jax import lax
from jax.experimental import pallas as pl
from jax.experimental.pallas import tpu as pltpu
from jax.sharding import PartitionSpec as P


NSIB = 4
HIGH = lax.Precision.HIGHEST
F32 = jnp.float32
BF16 = jnp.bfloat16
NT = (((1,), (1,)), ((), ()))
NN = (((1,), (0,)), ((), ()))


def dot_high(a, b, dims=NN):
    return lax.dot_general(a, b, dims, precision=HIGH, preferred_element_type=F32)


def dot_bf16(a, b, dims=NN):
    return lax.dot_general(a, b, dims, preferred_element_type=F32)


def split2(x):
    hi = x.astype(BF16)
    return hi, (x - hi.astype(F32)).astype(BF16)


def split3(x):
    hi = x.astype(BF16)
    rest = x - hi.astype(F32)
    mid = rest.astype(BF16)
    return hi, mid, (rest - mid.astype(F32)).astype(BF16)


def dot3(a, b, dims=NN):
    ah, al = split2(a)
    bh, bl = split2(b)
    return dot_bf16(ah, bh, dims) + (dot_bf16(ah, bl, dims) + dot_bf16(al, bh, dims))


def iota(shape, dim):
    return lax.broadcasted_iota(jnp.int32, shape, dim)


def spread(x, lane):
    return jnp.take_along_axis(x, jnp.full(x.shape, lane, jnp.int32), axis=1)


def eliminate_rows(panels, nexts, base):
    shape = panels[0].shape
    lane, sub = iota(shape, 1), iota(shape, 0)
    panels, nexts = list(panels), list(nexts)
    columns = [[spread(panel, base + t) for t in range(8)] for panel in panels]
    next_columns = [[spread(rows, base + t) for t in range(8)] for rows in nexts]
    inverses = [jnp.ones(shape, F32) for _ in panels]
    for t in range(8):
        here = lane == base + t
        one = (sub == t).astype(F32)
        for b, panel in enumerate(panels):
            column = columns[b][t]
            inverse = 1.0 / jnp.broadcast_to(column[t : t + 1, :], shape)
            inverses[b] = jnp.where(sub == t, inverse, inverses[b])
            ratio = jnp.where(sub > t, column, 0.0) * inverse
            row = jnp.where(here, 1.0, jnp.broadcast_to(panel[t : t + 1, :], shape))
            if nexts:
                next_ratio = next_columns[b][t] * inverse
            for u in range(t + 1, 8):
                later = columns[b][u]
                pivot_row = jnp.broadcast_to(later[t : t + 1, :], shape)
                columns[b][u] = later - ratio * pivot_row
                if nexts:
                    next_columns[b][u] = next_columns[b][u] - next_ratio * pivot_row
            panels[b] = jnp.where(here, one, panel) - ratio * row
            if nexts:
                nexts[b] = jnp.where(here, 0.0, nexts[b]) - next_ratio * row
    return panels, nexts, inverses


def invert_cholesky(blocks):
    count, size, span = len(blocks), blocks[0].shape[0], 32
    shape = (8, size)
    lane, sub = iota(shape, 1), iota(shape, 0)
    rows = [[block[8 * g : 8 * g + 8, :] for g in range(size // 8)] for block in blocks]
    out = [[] for _ in blocks]
    for start in range(0, size, span):
        end = start + span
        finals, scaled_rows = [[] for _ in blocks], [[] for _ in blocks]
        for g in range(start // 8, end // 8):
            base = 8 * g
            nexts = [rows[b][g + 1] for b in range(count)] if base + 8 < end else []
            panels, nexts, inverses = eliminate_rows([r[g] for r in rows], nexts, base)
            for b in range(count):
                panel = panels[b]
                scaled = panel * inverses[b]
                beyond = lane > sub + base
                out[b].append(jnp.where(beyond, 0.0, panel * jnp.sqrt(inverses[b])))
                finals[b].append(panel)
                scaled_rows[b].append(jnp.where(beyond & (lane < end), 0.0, scaled))
                if not nexts:
                    continue
                rows[b][g + 1] = nexts[b]
                scaled = jnp.where(beyond & (lane < base + 8), 0.0, scaled)
                clear = (lane >= base) & (lane < base + 8)
                for i in range(g + 2, end // 8):
                    terms = [
                        jnp.take_along_axis(
                            jnp.broadcast_to(panel[t : t + 1, :], shape), 8 * i + sub, axis=1
                        )
                        * jnp.broadcast_to(scaled[t : t + 1, :], shape)
                        for t in range(8)
                    ]
                    while len(terms) > 1:
                        terms = [terms[j] + terms[j + 1] for j in range(0, len(terms), 2)]
                    rows[b][i] = jnp.where(clear, 0.0, rows[b][i]) - terms[0]
        if end < size:
            clear = (lane >= start) & (lane < end)
            for b in range(count):
                factors = jnp.concatenate(finals[b], axis=0).T[end:]
                update = dot_high(factors, jnp.concatenate(scaled_rows[b], axis=0))
                for i in range(end // 8, size // 8):
                    k = 8 * i - end
                    rows[b][i] = jnp.where(clear, 0.0, rows[b][i]) - update[k : k + 8]
    return [jnp.concatenate(parts, axis=0) for parts in out]


def pick_lanes(x, order):
    rows, width = x.shape
    chunks = [x[:, 128 * q : 128 * (q + 1)] for q in range(width // 128)]
    parts = []
    for q in range(width // 128):
        wanted = jnp.broadcast_to(order[:, 128 * q : 128 * (q + 1)], (rows, 128))
        lane, chunk = wanted & 127, wanted >> 7
        picked = jnp.take_along_axis(chunks[0], lane, axis=1)
        for c in range(1, len(chunks)):
            picked = jnp.where(chunk == c, jnp.take_along_axis(chunks[c], lane, axis=1), picked)
        parts.append(picked)
    return jnp.concatenate(parts, axis=1)


def one_hot_rows(order, rows, width):
    column = jnp.broadcast_to(order.astype(F32), (128, order.shape[1])).T
    lanes = iota((rows, 128), 1).astype(F32)
    return jnp.concatenate(
        [(column[:rows] == lanes + 128.0 * q).astype(F32) for q in range(width // 128)], axis=1
    )


def factor_kernel(
    blocks_hbm,
    orders_hbm,
    interp_hbm,
    high_ref,
    low_ref,
    own_ref,
    blocks_ref,
    orders_ref,
    interp_ref,
    work,
    aug,
    sems,
):
    count, dof, _ = blocks_ref.shape
    skel, red = interp_ref.shape[1:]
    order_copy = pltpu.make_async_copy(orders_hbm, orders_ref, sems.at[0])
    block_copy = lambda b: pltpu.make_async_copy(
        blocks_hbm.at[b], blocks_ref.at[b], sems.at[1 + b]
    )
    interp_copy = lambda b: pltpu.make_async_copy(
        interp_hbm.at[b], interp_ref.at[b], sems.at[1 + count + b]
    )
    order_copy.start()
    for b in range(count):
        block_copy(b).start()
        interp_copy(b).start()
    order_copy.wait()

    @pl.loop(0, count)
    def _(b):
        order = orders_ref[pl.ds(b, 1), :]
        block_copy(b).wait()
        ordered = pick_lanes(pick_lanes(blocks_ref[b], order).T, order)
        interp_copy(b).wait()
        a_ss = ordered[:skel, :skel]
        a_sr = ordered[:skel, skel:]
        interp = interp_ref[b]
        interp_t = interp.T
        bar_sr = a_sr - dot_high(a_ss, interp)
        left = jnp.concatenate([a_sr.T, interp_t], axis=1)
        right = jnp.concatenate([interp, bar_sr], axis=0)
        work[b] = ordered[skel:, skel:] - dot_high(left, right)
        place = one_hot_rows(order, dof, dof)
        place_s = place[:skel].astype(BF16)
        pieces = [dot_bf16(part, place_s) for part in split3(interp_t)]
        aug[b, :, :dof] = place[skel:] - (pieces[0] + (pieces[1] + pieces[2]))
        aug[b, :, dof:] = bar_sr.T
        own_ref[b] = a_ss

    panels = red // 128
    for k in range(panels):
        lo, hi = 128 * k, 128 * (k + 1)
        inverses = invert_cholesky([work[b, lo:hi, lo:hi] for b in range(count)])
        for b in range(count):
            solved = dot3(inverses[b], aug[b, lo:hi, :])
            aug[b, lo:hi, :] = solved
            if hi < red:
                panel = dot_high(work[b, hi:, lo:hi], inverses[b], NT)
                work[b, hi:, hi:] = work[b, hi:, hi:] - dot_high(panel, panel, NT)
                aug[b, hi:, :] = aug[b, hi:, :] - dot3(panel, solved)
    for b in range(count):
        solved_t = aug[b, :, dof:].T
        own_ref[b] = own_ref[b] - dot_high(solved_t, aug[b, :, dof:])
        grid_high, grid_low = split2(aug[b, :, :dof])
        high_ref[b, :red] = grid_high
        low_ref[b, :red] = grid_low
        place_s = one_hot_rows(orders_ref[b : b + 1, :], skel, dof)
        last_high, last_low = split2(place_s - dot3(solved_t, aug[b, :, :dof]))
        high_ref[b, red:] = last_high
        low_ref[b, red:] = last_low


def factor(self_blocks, orders, interpolation, interpret=False):
    count, dof, _ = self_blocks.shape
    skel, red = interpolation.shape[1:]
    return pl.pallas_call(
        factor_kernel,
        out_shape=(
            jax.ShapeDtypeStruct((count, dof, dof), BF16),
            jax.ShapeDtypeStruct((count, dof, dof), BF16),
            jax.ShapeDtypeStruct((count, skel, skel), F32),
        ),
        in_specs=[pl.BlockSpec(memory_space=pltpu.HBM)] * 3,
        scratch_shapes=[
            pltpu.VMEM((count, dof, dof), F32),
            pltpu.VMEM((count, dof), jnp.int32),
            pltpu.VMEM((count, skel, red), F32),
            pltpu.VMEM((count, red, red), F32),
            pltpu.VMEM((count, red, dof + skel), F32),
            pltpu.SemaphoreType.DMA((2 * count + 1,)),
        ],
        compiler_params=pltpu.CompilerParams(vmem_limit_bytes=51 << 20),
        cost_estimate=pl.CostEstimate(flops=8 << 30, bytes_accessed=6 << 20, transcendentals=0),
        interpret=interpret,
        name="factor",
    )(*[
        pltpu.with_memory_space_constraint(x, pltpu.HBM)
        for x in (self_blocks, orders, interpolation)
    ])


def pack_symmetric(block, flag):
    half = block.shape[0] // 2
    top, bottom = block[:half], block[half:]
    lane, row = iota((half, 128), 1), iota((half, 128), 0)
    turned = pltpu.roll(bottom, half, 1)
    body = jnp.where((lane >= half) | (lane > row), top, turned)
    diagonal = jnp.sum(jnp.where(lane == row, top, 0.0), axis=0, keepdims=True)
    return body, jnp.where(iota((1, 128), 1) < half, diagonal, flag)


def unpack_symmetric(body, tail):
    half = 64
    lane, row = iota((half, 128), 1), iota((half, 128), 0)
    upper = jnp.where((lane >= half) | (lane > row), body, 0.0)
    inner = jnp.where(lane < half, body, 0.0)
    lower = pltpu.roll(jnp.where(lane < row, inner, 0.0), half, 1)
    strict = jnp.concatenate([upper, lower], axis=0)
    first = jnp.where(lane == row, jnp.broadcast_to(tail, (half, 128)), 0.0)
    second = pltpu.roll(jnp.where(lane == row, inner, 0.0), half, 1)
    return strict + strict.T + jnp.concatenate([first, second], axis=0)


Y, Z, C = 4, 8, 2
STAGES = [(dy, dc) for dy in range(Y) for dc in range(C)]
TABLE = 128


def place_of(box):
    return box // (Z * C), box // C % Z, box % C


def box_of(y, z, c):
    return (y % Y * Z + z % Z) * C + c % C


def plan(boxes, reach):
    steps = [(j * (boxes // 2)) // reach for j in range(1, reach + 1)]
    steps += [boxes - (j * ((boxes - 1) // 2)) // reach for j in range(1, reach + 1)]
    lists = []
    for box in range(boxes):
        y, z, c = place_of(box)
        by_stage = {stage: [] for stage in STAGES}
        for step in steps:
            ty, tz, tc = place_of((box + step) % boxes)
            by_stage[(ty - y) % Y, (tc - c) % C].append((step, (tz - z) % Z))
        lists.append(by_stage)
    caps = [max(len(found[stage]) for found in lists) for stage in STAGES]
    starts = np.concatenate([[0], np.cumsum(caps)]).tolist()
    table = np.zeros((boxes, TABLE), np.int32)
    for box in range(boxes):
        y, z, c = place_of(box)
        for s, stage in enumerate(STAGES):
            for j, (step, _) in enumerate(lists[box][stage]):
                table[box, step] = starts[s] + j
            source = lists[box_of(y - stage[0], z, c - stage[1])]
            for j, (_, shift) in enumerate(source[stage]):
                table[box, boxes + starts[s] + j] = shift
    return table, caps, starts


def row_spec(table):
    return pl.BlockSpec(
        (8, table.shape[1]), lambda *args: (args[-1][0] // 8, 0), memory_space=pltpu.SMEM
    )


def gram(z_t):
    high, low = split2(z_t)
    return dot_bf16(high, high, NT) + (dot_bf16(high, low, NT) + dot_bf16(low, high, NT))


def slot_updates(high, low, slot_pair):
    both = gram((dot_bf16(high, slot_pair) + dot_bf16(low, slot_pair)).T)
    return both[:128, :128], both[128:, 128:]


def far_kernel(ids_ref, where_ref, table_ref, high_ref, low_ref, w_ref, *rest, caps, starts, boxes):
    outs, (bodies, tails) = rest[: len(caps)], rest[len(caps) :]
    parent = where_ref[0]
    bodies[...] = jnp.zeros_like(bodies)
    tails[...] = jnp.zeros_like(tails)
    count, _, slots, _ = w_ref.shape
    for box in range(count):
        by_slot = jnp.swapaxes(w_ref[box], 0, 1)
        for first in range(NSIB, slots, 2):
            pair = jnp.concatenate([by_slot[first], by_slot[first + 1]], axis=1)
            for s, update in enumerate(slot_updates(high_ref[box], low_ref[box], pair)):
                other = ids_ref[box, first + s]
                body, tail = pack_symmetric(update, (other & 1).astype(F32))
                place = table_ref[parent & 7, ((other >> 3) - parent) & (boxes - 1)]
                bodies[place] = body
                tails[pl.ds(place, 1), :] = tail
    for s, out in enumerate(outs):
        for j in range(caps[s]):
            out[64 * j : 64 * j + 64] = bodies[starts[s] + j]
        out[64 * caps[s] : 64 * caps[s] + 8] = jnp.concatenate(
            [tails[starts[s] : starts[s] + caps[s]], jnp.zeros((8 - caps[s], 128), F32)], axis=0
        )


def far_updates(ids, where, table, high, low, w, caps, starts, boxes, interpret=False):
    count, dof, _, skel = w.shape
    red = dof - skel
    whole = lambda shape: pl.BlockSpec(shape, lambda b, *_: (0,) * len(shape))
    outs = [(64 * cap + 8, 128) for cap in caps]
    return pl.pallas_call(
        functools.partial(far_kernel, caps=caps, starts=starts, boxes=boxes),
        out_shape=[jax.ShapeDtypeStruct(shape, F32) for shape in outs],
        grid_spec=pltpu.PrefetchScalarGridSpec(
            num_scalar_prefetch=2,
            grid=(1,),
            in_specs=[row_spec(table)]
            + [whole((count, red, dof)), whole((count, red, dof)), whole(w.shape)],
            out_specs=[whole(shape) for shape in outs],
            scratch_shapes=[
                pltpu.VMEM((starts[-1], 64, 128), F32),
                pltpu.VMEM((-(-starts[-1] // 8) * 8, 128), F32),
            ],
        ),
        compiler_params=pltpu.CompilerParams(vmem_limit_bytes=28 << 20),
        cost_estimate=pl.CostEstimate(flops=6 << 30, bytes_accessed=8 << 20, transcendentals=0),
        interpret=interpret,
        name="far_updates",
    )(ids, where, table, high, low, w)


def near_kernel(ids_ref, where_ref, high_ref, low_ref, w_ref, near_ref, *sib_outs):
    this_sib = where_ref[1]
    red = high_ref.shape[1] - w_ref.shape[3]
    count = w_ref.shape[0]
    sib = sib_outs[-1]
    sib[...] = jnp.zeros_like(sib)

    found = []
    for box in range(count):
        by_slot = jnp.swapaxes(w_ref[box, :, :8], 0, 1)
        for first in range(0, NSIB, 2):
            pair = jnp.concatenate([by_slot[first], by_slot[first + 1]], axis=1)
            product = dot_bf16(high_ref[box], pair) + dot_bf16(low_ref[box], pair)
            found.append((box, first, product[red:], gram(product[:red].T)))
    for box, first, last, both in found:
        for s in range(2):
            part = slice(128 * s, 128 * (s + 1))
            coupled = last[:, part]
            near_ref[box, first + s] = coupled
            other = ids_ref[box, first + s]
            child = other & 1
            body, tail = pack_symmetric(both[part, part], child.astype(F32))
            place = ((((other >> 1) & 3) - this_sib) & 3) * 2 + child
            rows = slice(128 * box, 128 * (box + 1))
            sib[place, rows, :] = coupled
            sib[place, 256:320, :] = sib[place, 256:320, :] + body
            sib[place, 320:321, :] = sib[place, 320:321, :] + tail

    for i, out in enumerate(sib_outs[:-1]):
        out[...] = sib[2 * i : 2 * i + 2]


def near_updates(ids, where, high, low, w, interpret=False):
    count, _, _, skel = w.shape
    return pl.pallas_call(
        near_kernel,
        out_shape=(
            [jax.ShapeDtypeStruct((count, NSIB, skel, skel), F32)]
            + [jax.ShapeDtypeStruct((2, 328, 128), F32)] * 4
        ),
        in_specs=[pl.BlockSpec(memory_space=pltpu.SMEM)] * 2
        + [pl.BlockSpec(memory_space=pltpu.VMEM)] * 3,
        out_specs=[pl.BlockSpec(memory_space=pltpu.VMEM)] * 5,
        scratch_shapes=[pltpu.VMEM((8, 328, 128), F32)],
        compiler_params=pltpu.CompilerParams(vmem_limit_bytes=28 << 20),
        cost_estimate=pl.CostEstimate(flops=3 << 30, bytes_accessed=8 << 20, transcendentals=0),
        interpret=interpret,
        name="near_updates",
    )(ids, where, high, low, w)


def couple_kernel(high_ref, low_ref, near_ref, w_ref, updated_ref):
    slots = w_ref.shape[2]
    by_slot = jnp.swapaxes(w_ref[0], 0, 1)
    parts = [near_ref[0, k].astype(BF16) for k in range(NSIB)]
    for first in range(NSIB, slots, 2):
        pair = jnp.concatenate([by_slot[first], by_slot[first + 1]], axis=1)
        coupled = dot_bf16(high_ref[0], pair) + dot_bf16(low_ref[0], pair)
        parts += [coupled[:, :128].astype(BF16), coupled[:, 128:].astype(BF16)]
    updated_ref[0] = jnp.swapaxes(jnp.stack(parts), 0, 1)


def couple(high, low, near, w, interpret=False):
    count, dof, slots, skel = w.shape
    by_box = lambda shape: pl.BlockSpec((1,) + shape, lambda b: (b,) + (0,) * len(shape))
    last = pl.BlockSpec((1, skel, dof), lambda b: (b, dof // skel - 1, 0))
    return pl.pallas_call(
        couple_kernel,
        out_shape=jax.ShapeDtypeStruct((count, skel, slots, skel), BF16),
        grid=(count,),
        in_specs=[last, last, by_box((NSIB, skel, skel)), by_box((dof, slots, skel))],
        out_specs=by_box((skel, slots, skel)),
        compiler_params=pltpu.CompilerParams(vmem_limit_bytes=28 << 20),
        cost_estimate=pl.CostEstimate(flops=2 << 30, bytes_accessed=6 << 20, transcendentals=0),
        interpret=interpret,
        name="couple",
    )(high, low, near, w)


def route_kernel(where_ref, table_ref, *rest, caps, starts, boxes):
    got, outs, sums = rest[: len(caps)], rest[len(caps) : -1], rest[-1]
    row = where_ref[0] & 7
    sums[...] = jnp.zeros_like(sums)
    for s, block in enumerate(got):
        for j in range(caps[s]):
            shift = table_ref[row, boxes + starts[s] + j]
            body = block[64 * j : 64 * j + 64]
            tail = block[64 * caps[s] + j : 64 * caps[s] + j + 1]
            second = tail[:, 64:65]
            share = jnp.broadcast_to(second, body.shape)
            row_share = jnp.broadcast_to(second, tail.shape)
            sums[shift, 0:64] = sums[shift, 0:64] + body * (1.0 - share)
            sums[shift, 64:128] = sums[shift, 64:128] + body * share
            sums[shift, 128:129] = sums[shift, 128:129] + tail * (1.0 - row_share)
            sums[shift, 129:130] = sums[shift, 129:130] + tail * row_share
    for out, shifts in zip(outs, ROUTES):
        for i, shift in enumerate(shifts):
            out[PAIR * i : PAIR * (i + 1)] = sums[shift]


PAIR = 136
ROUTES = ((0,), (1, 3), (7, 5), (4,), (2,), (6,))


def route(where, table, got, caps, starts, boxes, interpret=False):
    whole = lambda shape: pl.BlockSpec(shape, lambda b, *_: (0,) * len(shape))
    outs = [(PAIR * len(shifts), 128) for shifts in ROUTES]
    return pl.pallas_call(
        functools.partial(route_kernel, caps=caps, starts=starts, boxes=boxes),
        out_shape=[jax.ShapeDtypeStruct(shape, F32) for shape in outs],
        grid_spec=pltpu.PrefetchScalarGridSpec(
            num_scalar_prefetch=1,
            grid=(1,),
            in_specs=[row_spec(table)] + [whole(block.shape) for block in got],
            out_specs=[whole(shape) for shape in outs],
            scratch_shapes=[pltpu.VMEM((Z, PAIR, 128), F32)],
        ),
        compiler_params=pltpu.CompilerParams(vmem_limit_bytes=16 << 20),
        cost_estimate=pl.CostEstimate(flops=1 << 22, bytes_accessed=2 << 20, transcendentals=0),
        interpret=interpret,
        name="route",
    )(where, table, *got)


def fold_kernel(up_ref, down_ref, two_ref, six_ref, out_two, out_six):
    out_two[...] = two_ref[...] + up_ref[PAIR:]
    out_six[...] = six_ref[...] + down_ref[PAIR:]


def fold(up, down, two, six, interpret=False):
    vmem = pl.BlockSpec(memory_space=pltpu.VMEM)
    return pl.pallas_call(
        fold_kernel,
        out_shape=[jax.ShapeDtypeStruct((PAIR, 128), F32)] * 2,
        in_specs=[vmem] * 4,
        out_specs=[vmem] * 2,
        compiler_params=pltpu.CompilerParams(vmem_limit_bytes=4 << 20),
        cost_estimate=pl.CostEstimate(flops=1 << 17, bytes_accessed=1 << 18, transcendentals=0),
        interpret=interpret,
        name="fold",
    )(up, down, two, six)


def assemble_kernel(where_ref, own_ref, *rest):
    far = rest[:-8]
    kept = rest[-8:-4]
    got = rest[-4:-1]
    out_ref = rest[-1]
    sibs = [kept[0]] + list(got)
    skeleton = []
    for c in range(2):
        body = sum(block[64 * c : 64 * c + 64] for block in far)
        tail = sum(block[128 + c : 129 + c] for block in far)
        for other in sibs:
            body = body + other[c, 256:320, :]
            tail = tail + other[c, 320:321, :]
        skeleton.append(own_ref[c] - unpack_symmetric(body, tail))
    here = where_ref[1]
    wide = lambda ref: jnp.concatenate([ref[0, 0:256, :], ref[1, 0:256, :]], axis=1)
    zero = jnp.zeros((128, 128), F32)
    first = wide(kept[0]) + jnp.concatenate(
        [
            jnp.concatenate([skeleton[0], zero], axis=1),
            jnp.concatenate([zero, skeleton[1]], axis=1),
        ],
        axis=0,
    )
    out_ref[:, pl.ds(pl.multiple_of(here * 256, 256), 256)] = 0.5 * (first + first.T)
    for s in range(1, 4):
        column = (here + 4 - s) & 3
        block = 0.5 * (wide(kept[4 - s]) + wide(got[s - 1]).T)
        out_ref[:, pl.ds(pl.multiple_of(column * 256, 256), 256)] = block


def assemble(where, own, far, kept, got, interpret=False):
    vmem = pl.BlockSpec(memory_space=pltpu.VMEM)
    args = [own, *far, *kept, *got]
    return pl.pallas_call(
        assemble_kernel,
        out_shape=jax.ShapeDtypeStruct((256, 1024), F32),
        in_specs=[pl.BlockSpec(memory_space=pltpu.SMEM)] + [vmem] * len(args),
        out_specs=vmem,
        compiler_params=pltpu.CompilerParams(vmem_limit_bytes=24 << 20),
        interpret=interpret,
        name="assemble",
    )(where, *args)


def on_device(self_blocks, orders, interpolation, couplings, neighbours):
    boxes = lax.axis_size("box")
    sibs = lax.axis_size("sib")
    parent, sib = lax.axis_index("box"), lax.axis_index("sib")
    count = orders.shape[1]
    slots = couplings.shape[3]
    where = jnp.stack([parent, sib]).astype(jnp.int32)
    plans, caps, starts = plan(boxes, (slots - NSIB) * count // 2)
    table = jnp.asarray(plans)
    high, low, own = factor(self_blocks[0], orders[0], interpolation[0])
    ids = neighbours[0]
    sent = far_updates(ids, where, table, high, low, couplings[0], caps, starts, boxes)

    def shifted(block, dy, dz, dc):
        moves = []
        for i in range(boxes):
            y, z, c = place_of(i)
            moves.append((i, box_of(y + dy, z + dz, c + dc)))
        return lax.ppermute(block, "box", moves)

    got = [sent[0]]
    for (dy, dc), block in zip(STAGES[1:], sent[1:]):
        got.append(shifted(block, dy, 0, dc))
    near, *kept = near_updates(ids, where, high, low, couplings[0])
    sib_got = []
    for s in range(1, sibs):
        moves = [(i, (i + s) % sibs) for i in range(sibs)]
        sib_got.append(lax.ppermute(kept[s], "sib", moves))
    here, up, down, four, two, six = route(where, table, got, caps, starts, boxes)
    up = shifted(up, 0, 1, 0)
    down = shifted(down, 0, -1, 0)
    four = shifted(four, 0, 4, 0)
    two, six = fold(up, down, two, six)
    two = shifted(two, 0, 2, 0)
    six = shifted(six, 0, -2, 0)
    far = [here, up, down, four, two, six]
    updated = couple(high, low, near, couplings[0])
    rows = assemble(where, own, far, kept, sib_got)
    return updated[None], rows[None]


def solution(mesh):
    return jax.shard_map(
        on_device,
        mesh=mesh,
        in_specs=(
            P("box", "sib", None, None),
            P("box", "sib", None),
            P("box", "sib", None, None),
            P("box", "sib", None, None, None),
            P("box", "sib", None),
        ),
        out_specs=(P("box", "sib", None, None, None), P("box", "sib", None)),
        check_vma=False,
    )
```
